256 devices in a mesh: sub: 32 (over y, z_lo, x), alt: 8 (over z_hi, core).
Axes of the slice: x: 4, y: 4, z: 8 (z_hi: 4, z_lo: 2; z = z_hi * 2 + z_lo), core: 2. Of those that a mesh axis runs over, the one named last changes fastest.
Arguments:
- cotangent: bfloat16 [4096, 4096], P('alt', 'sub'), may hold values from -180 to 180, as said below
- amplitude: bfloat16 [1024, 4096], P('alt', 'sub'), may hold values from 0.19921875 to 1
- phase: float32 [1024, 4096], P('alt', 'sub'), may hold values from -6 to 6
- position: float32 [2, 4096], P(None, 'sub'), may hold values from -1 to 1
- profile: float32 [16], P('alt'), may hold values from 0.35 to 15, as said below
- alt_weight: float32 [16], P('alt'), may hold values from 0.3 to 3
Outputs:
- phase_grad: float32 [1024, 4096], P('alt', 'sub')
- profile_grad: float32 [16], P('alt')
The draws below stay inside these ranges and needn't reach their ends.
Inputs may be any that keep to these rules, and one draw needn't show every extreme that they name: `cotangent`: cotangent values of varying scale per subaperture. `profile`: positive sodium densities.
All inputs are finite; a program needn't handle non-finite values.
Results may differ from the reference program's by a relative error of at most 0.0003.
Values may be sent and summed in bfloat16 or wider, within the bound.
A program may use at most 64 MiB of HBM per device.

```python
import math
import jax
import jax.numpy as jnp
from jax import lax

P_SIZE = 32
FIELD = 64
NSUB = 4096
NBINS = 16


def draw_cotangent(key, part):
    key_a = jax.random.fold_in(key, 11)
    key_b = jax.random.fold_in(key, 12)
    ramp = jnp.arange(NSUB, dtype=jnp.float32) / (NSUB - 1)
    spread = jnp.exp(jax.random.uniform(key_b, (NSUB,), jnp.float32) * jnp.log(10.0))
    base = jnp.clip(jax.random.normal(key_a, (FIELD * FIELD, NSUB), jnp.float32), -6.0, 6.0)
    values = base * (3.0 ** ramp * spread)[None, :]
    return values.astype(jnp.bfloat16)


def draw_profile(key, part):
    key_a = jax.random.fold_in(key, 21)
    ramp = jnp.arange(NBINS, dtype=jnp.float32) / (NBINS - 1)
    values = 3.0 ** ramp * jnp.exp(jax.random.uniform(key_a, (NBINS,), jnp.float32, -1.0, 1.0))
    return values


def level_of(own_key, shape, cuts, smallest, top_value):
    def one(dim, parts):
        heights = jax.random.uniform(jax.random.fold_in(jax.random.fold_in(own_key, 6), dim), (parts,), jnp.float32, smallest / len(cuts), top_value / len(cuts))
        return jnp.repeat(jnp.exp(heights), shape[dim] // parts).reshape((-1,) + (1,) * (len(shape) - dim - 1))

    level = one(*cuts[0])
    for cut in cuts[1:]:
        level = level * one(*cut)
    return level


def bell_draw(rng, dims, deviation, most, split=(), kind=jnp.bfloat16):
    values = jax.random.normal(rng, dims, jnp.float32) * deviation
    if len(split) > 0:
        values = level_of(rng, dims, split, -0.22, 0.18) * values
    return jnp.clip(values, min=-most, max=most).astype(kind)


def setup_inputs(seed: int = 0) -> dict:
    key_list = jax.random.split(jax.random.key(seed), 7)
    cotangent = draw_cotangent(jax.random.fold_in(key_list[6], 71), 0)
    amplitude = jnp.clip(0.19921875 + 0.80078125 * jax.random.uniform(key_list[1], (P_SIZE * P_SIZE, NSUB), jnp.float32) ** level_of(key_list[1], (P_SIZE * P_SIZE, NSUB), ((0, 8), (1, 32)), -0.2, 0.2), 0.19921875, 1.0).astype(jnp.bfloat16)
    phase = bell_draw(key_list[2], (P_SIZE * P_SIZE, NSUB), 1.0, 6.0, ((0, 8), (1, 32)), jnp.float32)
    position = jnp.clip(jax.random.uniform(key_list[3], (2, NSUB), jnp.float32, -1.0, 1.0) * level_of(key_list[3], (2, NSUB), ((1, 32),), -0.4, 0.0), -1.0, 1.0)
    profile = draw_profile(jax.random.fold_in(key_list[6], 71), 0)
    alt_weight = jnp.clip(jnp.exp(math.log(3.0) - 2.3025851 * jax.random.uniform(key_list[5], (NBINS,), jnp.float32) ** level_of(key_list[5], (NBINS,), ((0, 8),), -0.2, 0.2)), 0.3, 3.0)
    return dict(cotangent=cotangent, amplitude=amplitude, phase=phase, position=position, profile=profile, alt_weight=alt_weight)


ELONG = 0.75

def dft_tables(size_pupil, size_field):
    rows = jnp.arange(size_field, dtype=jnp.int32)[:, None]
    cols = jnp.arange(size_pupil, dtype=jnp.int32)[None, :]
    angle = 2.0 * jnp.pi / size_field * (rows * cols % size_field).astype(jnp.float32)
    return (jnp.cos(angle), -jnp.sin(angle))

def spot_image(psi, ampl, table_re, table_im, size_pupil):
    high = lax.Precision.HIGHEST
    field_re = ampl * jnp.cos(psi)
    field_im = ampl * jnp.sin(psi)
    first_re = jnp.einsum('kj,ajs->aks', table_re, field_re, precision=high) - jnp.einsum('kj,ajs->aks', table_im, field_im, precision=high)
    first_im = jnp.einsum('kj,ajs->aks', table_re, field_im, precision=high) + jnp.einsum('kj,ajs->aks', table_im, field_re, precision=high)
    final_re = jnp.einsum('ka,ams->kms', table_re, first_re, precision=high) - jnp.einsum('ka,ams->kms', table_im, first_im, precision=high)
    final_im = jnp.einsum('ka,ams->kms', table_re, first_im, precision=high) + jnp.einsum('ka,ams->kms', table_im, first_re, precision=high)
    return (final_re * final_re + final_im * final_im) / (size_pupil * size_pupil)

def reference(cotangent, amplitude, phase, position, profile, alt_weight):
    nsub_all = phase.shape[1]
    nbins_all = profile.shape[0]
    grad_img = cotangent.astype(jnp.float32).reshape(FIELD, FIELD, nsub_all)
    ampl = amplitude.astype(jnp.float32).reshape(P_SIZE, P_SIZE, nsub_all)
    phases = phase.reshape(P_SIZE, P_SIZE, nsub_all)
    table_re, table_im = dft_tables(P_SIZE, FIELD)
    coord = jnp.arange(P_SIZE, dtype=jnp.float32) - (P_SIZE - 1) / 2.0
    tilt = coord[None, :, None] * position[0][None, None, :] + coord[:, None, None] * position[1][None, None, :]
    total = jnp.sum(profile)

    def step(accum, index):
        kappa = ELONG * (2.0 * index.astype(jnp.float32) / (nbins_all - 1) - 1.0)
        psi = phases + kappa * tilt
        intensity, pull = jax.vjp(lambda value: spot_image(value, ampl, table_re, table_im, P_SIZE), psi)
        dpsi, = pull(profile[index] * alt_weight[index] * grad_img)
        stat = jnp.sum(grad_img * intensity)
        return (accum + dpsi, stat)
    accum, stats = lax.scan(step, jnp.zeros((P_SIZE, P_SIZE, nsub_all), jnp.float32), jnp.arange(nbins_all, dtype=jnp.int32))
    phase_grad = (accum / total).reshape(P_SIZE * P_SIZE, nsub_all)
    centre = jnp.sum(profile * alt_weight * stats)
    profile_grad = (alt_weight * stats / total - centre / (total * total)) / nsub_all
    return (phase_grad, profile_grad)
```

```python
import functools

import jax
import jax.numpy as jnp
import numpy as np
from jax import lax
from jax.experimental import pallas as pl
from jax.experimental.pallas import tpu as pltpu
from jax.sharding import PartitionSpec as P

F32 = jnp.float32
BF16 = jnp.bfloat16
MESH = pl.DeviceIdType.MESH

N_PUPIL = 32
N_FIELD = 64
N_BINS = 16
N_ALT = 8
LANES = 128


def split_np(m):
    hi = np.asarray(m, np.float32).astype(BF16)
    lo = (np.asarray(m, np.float64) - hi.astype(np.float64)).astype(np.float32).astype(BF16)
    return hi, lo


def make_tables():
    n = np.arange(N_FIELD)
    angle = 2.0 * np.pi / N_FIELD * (np.outer(n, n) % N_FIELD)
    cos, sin = np.cos(angle), np.sin(angle)
    eye = np.eye(4)
    half_c, half_s = cos[:, :N_PUPIL], sin[:, :N_PUPIL]
    kc, ks = np.kron(eye, half_c), np.kron(eye, half_s)
    w1 = np.block([[kc.T, -ks.T], [ks.T, kc.T]])
    w3 = np.block([[kc, ks]])
    w4 = w3.T
    w5 = np.block([[kc, ks], [-ks, kc]])
    a2 = np.block([[half_c, half_s], [-half_s, half_c]])
    a3 = np.vstack([cos, sin])
    a5 = np.block([[cos[:N_PUPIL], -sin[:N_PUPIL]], [sin[:N_PUPIL], cos[:N_PUPIL]]])
    out = []
    for w in (w1, w3, w4, w5):
        out += list(split_np(w))
    for a in (a2, a3, a5):
        hi, lo = split_np(a)
        out.append(np.concatenate([hi, hi, lo], axis=1))
    return out


def split(x):
    hi = x.astype(BF16)
    return hi, (x - hi.astype(F32)).astype(BF16)


def mm(a, b):
    return jnp.dot(a, b, preferred_element_type=F32)


def lane_mm(x, w_hi, w_lo):
    hi, lo = split(x)
    rows = x.shape[0]
    both = mm(jnp.concatenate([hi, lo], axis=0), w_hi)
    return both[:rows] + both[rows:] + mm(hi, w_lo)


def row_mm(table, x):
    hi, lo = split(x)
    return mm(table, jnp.concatenate([hi, lo, hi], axis=0))


def sincos(x):
    n = jnp.floor(x * (2.0 / np.pi) + 0.5)
    r = x - n * 1.5703125
    r = r - n * 4.837512969970703125e-4
    r = r - n * 7.54978995489188216e-8
    z = r * r
    s = ((-1.9515295891e-4 * z + 8.3321608736e-3) * z - 1.6666654611e-1) * z * r + r
    c = ((2.443315711809948e-5 * z - 1.388731625493765e-3) * z + 4.166664568298827e-2) * z * z - 0.5 * z + 1.0
    q = n.astype(jnp.int32)
    odd = (q & 1) == 1
    sv = jnp.where(odd, c, s)
    cv = jnp.where(odd, s, c)
    sv = jnp.where((q & 2) == 2, -sv, sv)
    cv = jnp.where(((q + 1) & 2) == 2, -cv, cv)
    return sv, cv


def swap4(x):
    lane = lax.broadcasted_iota(jnp.int32, x[0].shape, 1)
    keep0 = ((lane // 4) % 2) == 0
    keep1 = ((lane // 8) % 2) == 0

    def pair(a, b, shift, keep):
        return (
            jnp.where(keep, a, pltpu.roll(b, shift, 1)),
            jnp.where(keep, pltpu.roll(a, LANES - shift, 1), b),
        )

    y0, y1 = pair(x[0], x[1], 4, keep0)
    y2, y3 = pair(x[2], x[3], 4, keep0)
    z0, z2 = pair(y0, y2, 8, keep1)
    z1, z3 = pair(y1, y3, 8, keep1)
    return z0, z1, z2, z3


def kernel(
    dims,
    cot_hbm, amp_hbm, ph_hbm, pos_ref, prof_ref, wt_ref,
    w1h_hbm, w1l_hbm, w3h_hbm, w3l_hbm, w4h_hbm, w4l_hbm, w5h_hbm, w5l_hbm, a2_hbm, a3_hbm, a5_hbm,
    out_ref, pg_ref,
    cot_in, amp_in, ph_in,
    w1h, w1l, w3h, w3l, w4h, w4l, w5h, w5l, a2, a3, a5,
    cot_send, amp_send, ph_send, small_send,
    cot_recv, amp_recv, ph_recv, small_recv,
    back_send, back_recv, st_a, st_b, row_a, row_b,
    yu, uf, bw, yg, cs, gf, qf, ct, sn, er, ei, sf,
    load_sem, send_sem, recv_sem, sa_send, sa_recv, sb_send, sb_recv,
):
    ny, nz, nx = dims
    me = lax.axis_index("alt")
    sub = lax.axis_index("sub")
    y, zl, x = sub // (nz * nx), (sub // nx) % nz, sub % nx

    plane = []
    for oy in range(ny):
        for ox in range(nx):
            if oy or ox:
                qy, qx = (y + oy) % ny, (x + ox) % nx
                plane.append(({"sub": qy * (nz * nx) + zl * nx + qx}, qy * nx + qx))
    column = []
    for oz in range(nz):
        for oa in range(N_ALT):
            if oz or oa:
                qz, qa = (zl + oz) % nz, (me + oa) % N_ALT
                column.append(({"sub": y * (nz * nx) + qz * nx + x, "alt": qa}, qz * N_ALT + qa))
    my_plane = y * nx + x
    my_column = zl * N_ALT + me

    loads = []
    for src, dst in (
        (ph_hbm, ph_in), (amp_hbm, amp_in), (cot_hbm, cot_in),
        (w1h_hbm, w1h), (w1l_hbm, w1l), (a2_hbm, a2), (w3h_hbm, w3h), (w3l_hbm, w3l), (a3_hbm, a3),
        (w4h_hbm, w4h), (w4l_hbm, w4l), (a5_hbm, a5), (w5h_hbm, w5h), (w5l_hbm, w5l),
    ):
        cp = pltpu.make_async_copy(src, dst, load_sem.at[len(loads)])
        cp.start()
        loads.append(cp)

    barrier = pltpu.get_barrier_semaphore()
    for device, _ in plane + column:
        pl.semaphore_signal(barrier, inc=1, device_id=device, device_id_type=MESH)

    row = lax.broadcasted_iota(jnp.int32, (8, LANES), 0)
    lane = lax.broadcasted_iota(jnp.int32, (8, LANES), 1)
    small = jnp.zeros((8, LANES), F32)
    for b in range(2):
        here = lane == 2 * me + b
        small = jnp.where(here & (row == 0), prof_ref[b], small)
        small = jnp.where(here & (row == 1), wt_ref[b], small)
    small_send[...] = small

    loads[0].wait()
    t = jnp.concatenate(swap4([ph_in[32 * k : 32 * k + 32, :] for k in range(4)]), axis=0).T
    ph_send[...] = t.reshape(8, 16, LANES)
    loads[1].wait()
    amp = amp_in[...].astype(F32)
    t = jnp.concatenate(swap4([amp[32 * k : 32 * k + 32, :] for k in range(4)]), axis=0).T
    amp_send[...] = t.reshape(8, 16, LANES).astype(BF16)

    pl.semaphore_wait(barrier, len(plane) + len(column))

    order = [4, 5, 2, 6, 3, 7, 1]
    kinds = ((small_send, small_recv), (ph_send, ph_recv), (amp_send, amp_recv), (cot_send, cot_recv), (back_send, back_recv))

    def exchange(kind, offset):
        src, dst = kinds[kind]
        peer = (me + offset) % N_ALT
        return pltpu.make_async_remote_copy(
            src_ref=src if kind == 0 else src.at[peer],
            dst_ref=dst.at[me],
            send_sem=send_sem.at[kind, peer],
            recv_sem=recv_sem.at[kind, me],
            device_id={"alt": peer},
            device_id_type=MESH,
        )

    def arrival(kind, offset):
        src, dst = kinds[kind]
        peer = (me + offset) % N_ALT
        return pltpu.make_async_remote_copy(
            src_ref=src if kind == 0 else src.at[peer],
            dst_ref=dst.at[peer],
            send_sem=send_sem.at[kind, peer],
            recv_sem=recv_sem.at[kind, peer],
            device_id={"alt": peer},
            device_id_type=MESH,
        )

    def start(kind):
        for offset in order:
            exchange(kind, offset).start()

    def wait_in(kind):
        for offset in order:
            arrival(kind, offset).wait_recv()

    def wait_out(kind):
        for offset in order:
            exchange(kind, offset).wait_send()

    start(0)
    start(1)
    start(2)

    loads[2].wait()
    for half in range(2):
        z = swap4([cot_in[256 * half + 64 * k : 256 * half + 64 * k + 64, :].astype(F32) for k in range(4)])
        for u in range(2):
            t = jnp.concatenate([z[2 * u], z[2 * u + 1]], axis=0).T
            cot_send[:, 16 * half : 16 * half + 16, LANES * u : LANES * u + LANES] = t.reshape(8, 16, LANES).astype(BF16)
    start(3)

    small_recv[me] = small
    ph_recv[me] = ph_send[me]
    amp_recv[me] = amp_send[me]
    cot_recv[me] = cot_send[me]

    src = lax.broadcasted_iota(jnp.int32, (LANES, 4 * LANES), 0)
    dst = lax.broadcasted_iota(jnp.int32, (LANES, 4 * LANES), 1)
    pick = (src == 16 * me + 4 * ((dst % LANES) // 32) + dst // LANES).astype(F32)
    pos = jnp.concatenate([pos_ref[...], jnp.zeros((6, LANES), F32)], axis=0)
    pos = jnp.dot(pos, pick, precision=lax.Precision.HIGHEST, preferred_element_type=F32)
    r64 = lax.broadcasted_iota(jnp.int32, (N_FIELD, LANES), 0)
    l64 = lax.broadcasted_iota(jnp.int32, (N_FIELD, LANES), 1)
    dr = jnp.where(r64 < 32, r64, r64 - N_FIELD).astype(F32)
    dc = (l64 % 32).astype(F32)
    twice = jnp.where(l64 % 32 == 0, 1.0, 2.0).astype(F32)
    for g in range(4):
        px = pos[0:1, LANES * g : LANES * g + LANES]
        py = pos[1:2, LANES * g : LANES * g + LANES]
        s, c = sincos(0.05 * (px * dc + py * dr))
        c2, s2 = c * c - s * s, 2.0 * s * c
        for j in range(8):
            ct[j, g], sn[j, g] = c, s
            if j < 7:
                c, s = c * c2 - s * s2, s * c2 + c * s2

    wait_in(0)
    bins = small_recv[0]
    for k in range(1, N_ALT):
        bins = bins + small_recv[k]
    prof, wt = bins[0:1, :], bins[1:2, :]
    total = jnp.sum(prof, axis=1, keepdims=True)
    omega = prof * wt / total
    for g in range(4):
        re = jnp.zeros((N_FIELD, LANES), F32)
        im = jnp.zeros((N_FIELD, LANES), F32)
        for j in range(8):
            up, down = omega[:, 8 + j : 9 + j], omega[:, 7 - j : 8 - j]
            re = re + (up + down) * ct[j, g]
            im = im - (up - down) * sn[j, g]
        sf[0, g] = re * twice
        sf[1, g] = im * twice

    for cp in loads[3:]:
        cp.wait()
    wait_in(1)
    wait_in(2)
    s, c = sincos(ph_recv[...].reshape(LANES, LANES))
    amp = amp_recv[...].astype(F32).reshape(LANES, LANES)
    e_re, e_im = amp * c, amp * s
    er[...] = e_re
    ei[...] = e_im
    yy = lane_mm(jnp.concatenate([e_re, e_im], axis=1), w1h[...], w1l[...])
    for k in range(4):
        yu[k] = yy[:, LANES * k : LANES * k + LANES]
    power = []
    for g in range(4):
        m = [yu.at[k][pl.ds(g, 32, stride=4), :] for k in range(4)]
        m = [jnp.concatenate([m[0], m[1]], axis=1), jnp.concatenate([m[2], m[3]], axis=1)]
        u = row_mm(a2[...], jnp.concatenate(m, axis=0))
        uf[g] = u
        power.append(u[:64] * u[:64] + u[64:] * u[64:])
    yb = lane_mm(jnp.concatenate(power, axis=0), w3h[...], w3l[...])
    keep = jnp.where(r64 == 32, 0.0, twice) * (1.0 / (1024.0 * 4096.0))
    for g in range(4):
        v = row_mm(a3[...], yb[64 * g : 64 * g + 64, :])
        bw[0, g] = (v[:64, :LANES] - v[64:, LANES:]) * keep
        bw[1, g] = (v[:64, LANES:] + v[64:, :LANES]) * keep

    wait_in(3)
    cot = cot_recv[...].reshape(256, 256)
    yy = mm(cot, w3h[...]) + mm(cot, w3l[...])
    yg[0], yg[1] = yy[:, :LANES], yy[:, LANES:]
    for g in range(4):
        m = [yg.at[k][pl.ds(g, 64, stride=4), :] for k in range(2)]
        v = row_mm(a3[...], jnp.concatenate(m, axis=1))
        g_re = v[:64, :LANES] - v[64:, LANES:]
        g_im = v[:64, LANES:] + v[64:, :LANES]
        b_re, b_im, s_re, s_im = bw[0, g], bw[1, g], sf[0, g], sf[1, g]
        qf[0, g] = g_re * b_re + g_im * b_im
        qf[1, g] = g_im * b_re - g_re * b_im
        gf[g] = jnp.concatenate([g_re * s_re - g_im * s_im, g_re * s_im + g_im * s_re], axis=1)

    sums = []
    for part, table in ((0, ct), (1, sn)):
        rows = []
        for j in range(8):
            acc = jnp.zeros((8, LANES), F32)
            for g in range(4):
                acc = acc + jnp.sum((qf[part, g] * table[j, g]).reshape(8, 8, LANES), axis=0)
            rows.append(jnp.sum(acc, axis=0, keepdims=True))
        sums.append(jnp.sum(jnp.concatenate(rows, axis=0), axis=1, keepdims=True))
    here = jnp.where(lane == 8 + row, sums[0] + sums[1], 0.0) + jnp.where(lane == 7 - row, sums[0] - sums[1], 0.0)
    mine = jnp.sum(here, axis=0, keepdims=True)
    row_a[...] = mine
    st_a[my_plane] = mine

    def plane_copy(device, slot, me_slot, src, dst, ss, rs):
        return pltpu.make_async_remote_copy(
            src_ref=src, dst_ref=dst.at[me_slot], send_sem=ss.at[slot], recv_sem=rs.at[me_slot],
            device_id=device, device_id_type=MESH,
        )

    def plane_arrival(device, slot, src, dst, ss, rs):
        return pltpu.make_async_remote_copy(
            src_ref=src, dst_ref=dst.at[slot], send_sem=ss.at[slot], recv_sem=rs.at[slot],
            device_id=device, device_id_type=MESH,
        )

    for device, slot in plane:
        plane_copy(device, slot, my_plane, row_a, st_a, sa_send, sa_recv).start()

    z = []
    for g in range(4):
        v = row_mm(a3[...], gf[g])
        z.append(jnp.concatenate([v[:64, :LANES] + v[64:, LANES:], v[:64, LANES:] - v[64:, :LANES]], axis=1))
    g_hat = lane_mm(jnp.concatenate(z, axis=0), w4h[...], w4l[...])
    for g in range(4):
        gh = g_hat[64 * g : 64 * g + 64, :]
        v = jnp.concatenate([uf[g, :64, :] * gh, uf[g, 64:, :] * gh], axis=0)
        v = row_mm(a5[...], v)
        for k in range(2):
            cs.at[k][pl.ds(g, 32, stride=4), :] = v[:32, LANES * k : LANES * k + LANES]
            cs.at[2 + k][pl.ds(g, 32, stride=4), :] = v[32:, LANES * k : LANES * k + LANES]
    conv = lane_mm(jnp.concatenate([cs[k] for k in range(4)], axis=1), w5h[...], w5l[...])
    grad = (er[...] * conv[:, LANES:] - ei[...] * conv[:, :LANES]) * (2.0 / (1024.0 * 4096.0))
    back_send[...] = grad.reshape(8, 16, LANES)
    start(4)
    back_recv[me] = back_send[me]

    for device, slot in plane:
        plane_arrival(device, slot, row_a, st_a, sa_send, sa_recv).wait_recv()
    acc = st_a[0]
    for k in range(1, ny * nx):
        acc = acc + st_a[k]
    row_b[...] = acc
    st_b[my_column] = acc
    for device, slot in column:
        plane_copy(device, slot, my_column, row_b, st_b, sb_send, sb_recv).start()

    wait_in(4)
    m = back_recv[...].reshape(LANES, LANES).T
    rows = swap4([m[32 * k : 32 * k + 32, :] for k in range(4)])
    for k in range(4):
        out_ref[32 * k : 32 * k + 32, :] = rows[k]

    for device, slot in column:
        plane_arrival(device, slot, row_b, st_b, sb_send, sb_recv).wait_recv()
    stat = st_b[0]
    for k in range(1, nz * N_ALT):
        stat = stat + st_b[k]
    centre = jnp.sum(prof * wt * stat, axis=1, keepdims=True)
    n_all = ny * nz * nx * LANES
    pg = (wt * stat / total - centre / (total * total)) * (1.0 / n_all)
    for b in range(2):
        pg_ref[b] = jnp.sum(jnp.where(lane[0:1] == 2 * me + b, pg, 0.0))

    for kind in range(5):
        wait_out(kind)
    for device, slot in plane:
        plane_copy(device, slot, my_plane, row_a, st_a, sa_send, sa_recv).wait_send()
    for device, slot in column:
        plane_copy(device, slot, my_column, row_b, st_b, sb_send, sb_recv).wait_send()


def local(dims, cotangent, amplitude, phase, position, profile, alt_weight):
    tables = make_tables()
    any_spec = pl.BlockSpec(memory_space=pl.ANY)
    vmem = pl.BlockSpec(memory_space=pltpu.VMEM)
    smem = pl.BlockSpec(memory_space=pltpu.SMEM)
    n_plane, n_column = dims[0] * dims[2], dims[1] * N_ALT
    table_scratch = [pltpu.VMEM(t.shape, BF16) for t in tables]
    dma = pltpu.SemaphoreType.DMA
    return pl.pallas_call(
        functools.partial(kernel, dims),
        out_shape=(jax.ShapeDtypeStruct((LANES, LANES), F32), jax.ShapeDtypeStruct((2,), F32)),
        in_specs=[any_spec] * 3 + [vmem, smem, smem] + [any_spec] * len(tables),
        out_specs=(vmem, smem),
        scratch_shapes=[
            pltpu.VMEM((512, LANES), BF16), pltpu.VMEM((LANES, LANES), BF16), pltpu.VMEM((LANES, LANES), F32),
            *table_scratch,
            pltpu.VMEM((8, 32, 256), BF16), pltpu.VMEM((8, 16, LANES), BF16), pltpu.VMEM((8, 16, LANES), F32), pltpu.VMEM((8, LANES), F32),
            pltpu.VMEM((8, 32, 256), BF16), pltpu.VMEM((8, 16, LANES), BF16), pltpu.VMEM((8, 16, LANES), F32), pltpu.VMEM((8, 8, LANES), F32),
            pltpu.VMEM((8, 16, LANES), F32), pltpu.VMEM((8, 16, LANES), F32),
            pltpu.VMEM((n_plane, 1, LANES), F32), pltpu.VMEM((n_column, 1, LANES), F32),
            pltpu.VMEM((1, LANES), F32), pltpu.VMEM((1, LANES), F32),
            pltpu.VMEM((4, LANES, LANES), F32), pltpu.VMEM((4, LANES, 256), F32), pltpu.VMEM((2, 4, 64, LANES), F32),
            pltpu.VMEM((2, 256, LANES), F32), pltpu.VMEM((4, LANES, LANES), F32), pltpu.VMEM((4, 64, 256), F32),
            pltpu.VMEM((2, 4, 64, LANES), F32),
            pltpu.VMEM((8, 4, 64, LANES), F32), pltpu.VMEM((8, 4, 64, LANES), F32),
            pltpu.VMEM((LANES, LANES), F32), pltpu.VMEM((LANES, LANES), F32),
            pltpu.VMEM((2, 4, 64, LANES), F32),
            dma((14,)), dma((5, 8)), dma((5, 8)), dma((n_plane,)), dma((n_plane,)), dma((n_column,)), dma((n_column,)),
        ],
        compiler_params=pltpu.CompilerParams(collective_id=0, has_side_effects=True),
    )(cotangent, amplitude, phase, position, profile, alt_weight, *[jnp.asarray(t) for t in tables])


def solution(mesh):
    dims = {32: (4, 2, 4), 2: (2, 1, 1)}[mesh.shape["sub"]]
    placed = (P("alt", "sub"), P("alt", "sub"), P("alt", "sub"), P(None, "sub"), P("alt"), P("alt"))
    return jax.shard_map(
        functools.partial(local, dims), mesh=mesh, in_specs=placed, out_specs=(P("alt", "sub"), P("alt")), check_vma=False
    )
```

```python
import functools

import jax
import jax.numpy as jnp
import numpy as np
from jax import lax
from jax.experimental import pallas as pl
from jax.experimental.pallas import tpu as pltpu
from jax.sharding import PartitionSpec as P

F32 = jnp.float32
BF16 = jnp.bfloat16
MESH = pl.DeviceIdType.MESH

N_PUPIL = 32
N_FIELD = 64
N_BINS = 16
N_ALT = 8
LANES = 128


def split_np(m):
    hi = np.asarray(m, np.float32).astype(BF16)
    lo = (np.asarray(m, np.float64) - hi.astype(np.float64)).astype(np.float32).astype(BF16)
    return hi, lo


def make_tables():
    n = np.arange(N_FIELD)
    angle = 2.0 * np.pi / N_FIELD * (np.outer(n, n) % N_FIELD)
    cos, sin = np.cos(angle), np.sin(angle)
    eye = np.eye(4)
    half_c, half_s = cos[:, :N_PUPIL], sin[:, :N_PUPIL]
    kc, ks = np.kron(eye, half_c), np.kron(eye, half_s)
    w1 = np.block([[kc.T, -ks.T], [ks.T, kc.T]])
    w3 = np.block([[kc, ks]])
    w4 = w3.T
    w5 = np.block([[kc, ks], [-ks, kc]])
    a2 = np.block([[half_c, half_s], [-half_s, half_c]])
    a3 = np.vstack([cos, sin])
    a5 = np.block([[cos[:N_PUPIL], -sin[:N_PUPIL]], [sin[:N_PUPIL], cos[:N_PUPIL]]])
    blocks = []
    for w in (w1[:, :256], w1[:, 256:], w3, w4, w5[:256], w5[256:]):
        blocks += list(split_np(w))
    for a in (a2, a3):
        hi, lo = split_np(a)
        blocks.append(np.concatenate([hi, hi, lo, np.zeros_like(lo)], axis=1))
    hi, lo = split_np(a5)
    blocks += [np.concatenate([hi, hi], axis=1), np.concatenate([lo, np.zeros_like(lo)], axis=1)]
    return np.concatenate(blocks, axis=0)


W1, W3, W4, W5 = (0, 512), 1024, 1536, (2048, 2560)
A2, A3, A5 = 3072, 3200, 3328


def split(x):
    hi = x.astype(BF16)
    return hi, (x - hi.astype(F32)).astype(BF16)


def mm(a, b):
    return jnp.dot(a, b, preferred_element_type=F32)


def lane_mm(parts, tab, row):
    rows = parts[0].shape[0]
    w_hi, w_lo = tab[row : row + 256, :], tab[row + 256 : row + 512, :]
    both = mm(jnp.concatenate(parts, axis=0), w_hi)
    return both[:rows] + both[rows:] + mm(parts[0], w_lo)


def row_mm(table, x):
    hi, lo = split(x)
    return mm(table, jnp.concatenate([hi, lo, hi], axis=0))


def sincos(x):
    n = jnp.floor(x * (2.0 / np.pi) + 0.5)
    r = x - n * 1.5703125
    r = r - n * 4.837512969970703125e-4
    r = r - n * 7.54978995489188216e-8
    z = r * r
    s = ((-1.9515295891e-4 * z + 8.3321608736e-3) * z - 1.6666654611e-1) * z * r + r
    c = ((2.443315711809948e-5 * z - 1.388731625493765e-3) * z + 4.166664568298827e-2) * z * z - 0.5 * z + 1.0
    q = n.astype(jnp.int32)
    odd = (q & 1) == 1
    sv = jnp.where(odd, c, s)
    cv = jnp.where(odd, s, c)
    sv = jnp.where((q & 2) == 2, -sv, sv)
    cv = jnp.where(((q + 1) & 2) == 2, -cv, cv)
    return sv, cv


def swap4(x):
    lane = lax.broadcasted_iota(jnp.int32, x[0].shape, 1)
    keep0 = ((lane // 4) % 2) == 0
    keep1 = ((lane // 8) % 2) == 0

    def pair(a, b, shift, keep):
        return (
            jnp.where(keep, a, pltpu.roll(b, shift, 1)),
            jnp.where(keep, pltpu.roll(a, LANES - shift, 1), b),
        )

    y0, y1 = pair(x[0], x[1], 4, keep0)
    y2, y3 = pair(x[2], x[3], 4, keep0)
    z0, z2 = pair(y0, y2, 8, keep1)
    z1, z3 = pair(y1, y3, 8, keep1)
    return z0, z1, z2, z3


def kernel(
    dims,
    cot_hbm, amp_hbm, ph_hbm, pos_hbm, prof_hbm, wt_hbm,
    tab_hbm,
    grad_ref, bins_ref,
    cot_in, amp_in, ph_in, pos_ref,
    tab, prof_ref, wt_ref,
    cot_send, amp_send, ph_send, small_send,
    cot_recv, amp_recv, ph_recv, small_recv,
    back_send, back_recv, st_a, st_b, row_a, row_b,
    yu, uf, bw, yg, cs, gf, qf, ct, sn, er, ei, sf,
    load_sem, send_sem, recv_sem, sems_a, sems_b,
):
    ny, nz, nx = dims
    me = lax.axis_index("alt")
    sub = lax.axis_index("sub")
    y, zl, x = sub // (nz * nx), (sub // nx) % nz, sub % nx

    plane = []
    for oy in range(ny):
        for ox in range(nx):
            if oy or ox:
                qy, qx = (y + oy) % ny, (x + ox) % nx
                plane.append({"sub": qy * (nz * nx) + zl * nx + qx})
    column = []
    for oz in range(nz):
        for oa in range(N_ALT):
            if oz or oa:
                qz, qa = (zl + oz) % nz, (me + oa) % N_ALT
                column.append({"sub": y * (nz * nx) + qz * nx + x, "alt": qa})
    my_plane = y * nx + x
    my_column = zl * N_ALT + me

    barrier = pltpu.get_barrier_semaphore()
    for device in plane + column:
        pl.semaphore_signal(barrier, inc=1, device_id=device, device_id_type=MESH)

    loads = []
    for src, dst in (
        (ph_hbm, ph_in), (amp_hbm, amp_in), (cot_hbm, cot_in), (pos_hbm, pos_ref),
        (prof_hbm, prof_ref), (wt_hbm, wt_ref), (tab_hbm, tab),
    ):
        cp = pltpu.make_async_copy(src, dst, load_sem.at[len(loads)])
        cp.start()
        loads.append(cp)

    loads[0].wait()
    t = jnp.concatenate(swap4([ph_in[32 * k : 32 * k + 32, :] for k in range(4)]), axis=0).T
    ph_send[...] = t.reshape(8, 16, LANES)
    loads[1].wait()
    amp = amp_in[...].astype(F32)
    t = jnp.concatenate(swap4([amp[32 * k : 32 * k + 32, :] for k in range(4)]), axis=0).T
    amp_send[...] = t.reshape(8, 16, LANES).astype(BF16)

    loads[4].wait()
    loads[5].wait()
    row = lax.broadcasted_iota(jnp.int32, (8, LANES), 0)
    lane = lax.broadcasted_iota(jnp.int32, (8, LANES), 1)
    small = jnp.zeros((8, LANES), F32)
    for b in range(2):
        here = lane == 2 * me + b
        small = jnp.where(here & (row == 0), prof_ref[b], small)
        small = jnp.where(here & (row == 1), wt_ref[b], small)
    small_send[...] = small

    pl.semaphore_wait(barrier, len(plane) + len(column))

    order = [(2, 0), (2, 1), (1, 0), (3, 0), (1, 1), (3, 1), (0, 1)]
    kinds = ((small_send, small_recv), (ph_send, ph_recv), (amp_send, amp_recv), (cot_send, cot_recv), (back_send, back_recv))

    def peer_of(offset):
        return (me // 2 + offset[0]) % (N_ALT // 2) * 2 + (me + offset[1]) % 2

    def exchange(kind, offset):
        src, dst = kinds[kind]
        peer = peer_of(offset)
        return pltpu.make_async_remote_copy(
            src_ref=src if kind == 0 else src.at[peer],
            dst_ref=dst.at[me],
            send_sem=send_sem.at[kind],
            recv_sem=recv_sem.at[kind],
            device_id={"alt": peer},
            device_id_type=MESH,
        )

    def start(kind):
        for offset in order:
            exchange(kind, offset).start()

    def wait_in(kind):
        dst = kinds[kind][1].at[pl.ds(0, N_ALT - 1)]
        pltpu.make_async_copy(dst, dst, recv_sem.at[kind]).wait()

    def wait_out(kind):
        dst = kinds[kind][1].at[pl.ds(0, N_ALT - 1)]
        pltpu.make_async_copy(dst, dst, send_sem.at[kind]).wait()

    start(0)
    start(1)
    start(2)

    loads[2].wait()
    for half in range(2):
        z = swap4([cot_in[256 * half + 64 * k : 256 * half + 64 * k + 64, :].astype(F32) for k in range(4)])
        for u in range(2):
            t = jnp.concatenate([z[2 * u], z[2 * u + 1]], axis=0).T
            cot_send[:, 16 * half : 16 * half + 16, LANES * u : LANES * u + LANES] = t.reshape(8, 16, LANES).astype(BF16)
    start(3)

    small_recv[me] = small
    ph_recv[me] = ph_send[me]
    amp_recv[me] = amp_send[me]
    cot_recv[me] = cot_send[me]

    src = lax.broadcasted_iota(jnp.int32, (LANES, 4 * LANES), 0)
    dst = lax.broadcasted_iota(jnp.int32, (LANES, 4 * LANES), 1)
    pick = (src == 16 * me + 4 * ((dst % LANES) // 32) + dst // LANES).astype(F32)
    loads[3].wait()
    pos = jnp.concatenate([pos_ref[...], jnp.zeros((6, LANES), F32)], axis=0)
    pos = jnp.dot(pos, pick, precision=lax.Precision.HIGHEST, preferred_element_type=F32)
    r64 = lax.broadcasted_iota(jnp.int32, (N_FIELD, LANES), 0)
    l64 = lax.broadcasted_iota(jnp.int32, (N_FIELD, LANES), 1)
    dr = jnp.where(r64 < 32, r64, r64 - N_FIELD).astype(F32)
    dc = (l64 % 32).astype(F32)
    twice = jnp.where(l64 % 32 == 0, 1.0, 2.0).astype(F32)
    for g in range(4):
        px = pos[0:1, LANES * g : LANES * g + LANES]
        py = pos[1:2, LANES * g : LANES * g + LANES]
        s, c = sincos(0.05 * (px * dc + py * dr))
        c2, s2 = c * c - s * s, 2.0 * s * c
        for j in range(8):
            ct[j, g], sn[j, g] = c, s
            if j < 7:
                c, s = c * c2 - s * s2, s * c2 + c * s2

    wait_in(0)
    bins = small_recv[0]
    for k in range(1, N_ALT):
        bins = bins + small_recv[k]
    prof, wt = bins[0:1, :], bins[1:2, :]
    total = jnp.sum(prof, axis=1, keepdims=True)
    omega = prof * wt / total
    for g in range(4):
        re = jnp.zeros((N_FIELD, LANES), F32)
        im = jnp.zeros((N_FIELD, LANES), F32)
        for j in range(8):
            up, down = omega[:, 8 + j : 9 + j], omega[:, 7 - j : 8 - j]
            re = re + (up + down) * ct[j, g]
            im = im - (up - down) * sn[j, g]
        sf[0, g] = re * twice
        sf[1, g] = im * twice

    loads[6].wait()
    wait_in(1)
    wait_in(2)
    s, c = sincos(ph_recv[...].reshape(LANES, LANES))
    amp = amp_recv[...].astype(F32).reshape(LANES, LANES)
    e_re, e_im = amp * c, amp * s
    er[...] = e_re
    ei[...] = e_im
    e_both = split(jnp.concatenate([e_re, e_im], axis=1))
    for h in range(2):
        half = lane_mm(e_both, tab, W1[h])
        yu[2 * h], yu[2 * h + 1] = half[:, :LANES], half[:, LANES:]
    a2, a3 = tab[A2 : A2 + LANES, :192], tab[A3 : A3 + LANES, :192]
    power = []
    for g in range(4):
        m = [yu.at[k][pl.ds(g, 32, stride=4), :] for k in range(4)]
        m = [jnp.concatenate([m[0], m[1]], axis=1), jnp.concatenate([m[2], m[3]], axis=1)]
        u = row_mm(a2, jnp.concatenate(m, axis=0))
        uf[g] = u
        power.append(u[:64] * u[:64] + u[64:] * u[64:])
    yb = lane_mm(split(jnp.concatenate(power, axis=0)), tab, W3)
    keep = jnp.where(r64 == 32, 0.0, twice) * (1.0 / (1024.0 * 4096.0))
    for g in range(4):
        v = row_mm(a3, yb[64 * g : 64 * g + 64, :])
        bw[0, g] = (v[:64, :LANES] - v[64:, LANES:]) * keep
        bw[1, g] = (v[:64, LANES:] + v[64:, :LANES]) * keep

    wait_in(3)
    cot = cot_recv[...].reshape(256, 256)
    yy = mm(cot, tab[W3 : W3 + 256, :]) + mm(cot, tab[W3 + 256 : W3 + 512, :])
    yg[0], yg[1] = yy[:, :LANES], yy[:, LANES:]
    for g in range(4):
        m = [yg.at[k][pl.ds(g, 64, stride=4), :] for k in range(2)]
        v = row_mm(a3, jnp.concatenate(m, axis=1))
        g_re = v[:64, :LANES] - v[64:, LANES:]
        g_im = v[:64, LANES:] + v[64:, :LANES]
        b_re, b_im, s_re, s_im = bw[0, g], bw[1, g], sf[0, g], sf[1, g]
        qf[0, g] = g_re * b_re + g_im * b_im
        qf[1, g] = g_im * b_re - g_re * b_im
        gf[g] = jnp.concatenate([g_re * s_re - g_im * s_im, g_re * s_im + g_im * s_re], axis=1)

    sums = []
    for part, table in ((0, ct), (1, sn)):
        rows = []
        for j in range(8):
            acc = jnp.zeros((8, LANES), F32)
            for g in range(4):
                acc = acc + jnp.sum((qf[part, g] * table[j, g]).reshape(8, 8, LANES), axis=0)
            rows.append(jnp.sum(acc, axis=0, keepdims=True))
        sums.append(jnp.sum(jnp.concatenate(rows, axis=0), axis=1, keepdims=True))
    here = jnp.where(lane == 8 + row, sums[0] + sums[1], 0.0) + jnp.where(lane == 7 - row, sums[0] - sums[1], 0.0)
    mine = jnp.sum(here, axis=0, keepdims=True)
    row_a[...] = mine
    st_a[my_plane] = mine

    def post(peers, me_slot, src, dst, sems):
        for device in peers:
            pltpu.make_async_remote_copy(
                src_ref=src, dst_ref=dst.at[me_slot], send_sem=sems.at[0], recv_sem=sems.at[1],
                device_id=device, device_id_type=MESH,
            ).start()

    def wait_all(peers, dst, sem):
        if peers:
            part = dst.at[pl.ds(0, len(peers))]
            pltpu.make_async_copy(part, part, sem).wait()

    post(plane, my_plane, row_a, st_a, sems_a)

    z = []
    for g in range(4):
        v = row_mm(a3, gf[g])
        z.append(jnp.concatenate([v[:64, :LANES] + v[64:, LANES:], v[:64, LANES:] - v[64:, :LANES]], axis=1))
    g_hat = lane_mm(split(jnp.concatenate(z, axis=0)), tab, W4)
    for g in range(4):
        gh = g_hat[64 * g : 64 * g + 64, :]
        v = jnp.concatenate([uf[g, :64, :] * gh, uf[g, 64:, :] * gh], axis=0)
        hi, lo = split(v)
        v = mm(tab[A5 : A5 + 64, :], jnp.concatenate([hi, lo], axis=0)) + mm(tab[A5 + 64 : A5 + 128, :LANES], hi)
        for k in range(2):
            cs.at[k][pl.ds(g, 32, stride=4), :] = v[:32, LANES * k : LANES * k + LANES]
            cs.at[2 + k][pl.ds(g, 32, stride=4), :] = v[32:, LANES * k : LANES * k + LANES]
    conv = sum(lane_mm(split(jnp.concatenate([cs[2 * h], cs[2 * h + 1]], axis=1)), tab, W5[h]) for h in range(2))
    grad = (er[...] * conv[:, LANES:] - ei[...] * conv[:, :LANES]) * (2.0 / (1024.0 * 4096.0))
    back_send[...] = grad.reshape(8, 16, LANES)
    start(4)
    back_recv[me] = back_send[me]

    wait_all(plane, st_a, sems_a.at[1])
    acc = st_a[0]
    for k in range(1, ny * nx):
        acc = acc + st_a[k]
    row_b[...] = acc
    st_b[my_column] = acc
    post(column, my_column, row_b, st_b, sems_b)

    wait_in(4)
    m = back_recv[...].reshape(LANES, LANES).T
    rows = swap4([m[32 * k : 32 * k + 32, :] for k in range(4)])
    for k in range(4):
        grad_ref[32 * k : 32 * k + 32, :] = rows[k]

    wait_all(column, st_b, sems_b.at[1])
    stat = st_b[0]
    for k in range(1, nz * N_ALT):
        stat = stat + st_b[k]
    bins_ref[...] = jnp.concatenate([prof, wt, stat, total * jnp.ones((1, LANES), F32), jnp.zeros((4, LANES), F32)], axis=0)

    for kind in range(5):
        wait_out(kind)
    wait_all(plane, st_a, sems_a.at[0])
    wait_all(column, st_b, sems_b.at[0])


def finish(n_all, grad_ref, bins_ref, out_hbm, pg_ref, sem):
    copy = pltpu.make_async_copy(grad_ref, out_hbm, sem)
    copy.start()
    me = lax.axis_index("alt")
    lane = lax.broadcasted_iota(jnp.int32, (1, LANES), 1)
    prof, wt, stat, total = (bins_ref[k : k + 1, :] for k in range(4))
    centre = jnp.sum(prof * wt * stat, axis=1, keepdims=True)
    pg = (wt * stat / total - centre / (total * total)) * (1.0 / n_all)
    for b in range(2):
        pg_ref[b] = jnp.sum(jnp.where(lane == 2 * me + b, pg, 0.0))
    copy.wait()


def local(dims, cotangent, amplitude, phase, position, profile, alt_weight):
    tables = jnp.asarray(make_tables())
    any_spec = pl.BlockSpec(memory_space=pl.ANY)
    vmem = pl.BlockSpec(memory_space=pltpu.VMEM)
    smem = pl.BlockSpec(memory_space=pltpu.SMEM)
    n_plane, n_column = dims[0] * dims[2], dims[1] * N_ALT
    dma = pltpu.SemaphoreType.DMA
    back, bins = pl.pallas_call(
        functools.partial(kernel, dims),
        out_shape=(pltpu.VMEM((LANES, LANES), F32), pltpu.VMEM((8, LANES), F32)),
        in_specs=[any_spec] * 7,
        out_specs=(vmem, vmem),
        scratch_shapes=[
            pltpu.VMEM((512, LANES), BF16), pltpu.VMEM((LANES, LANES), BF16), pltpu.VMEM((LANES, LANES), F32), pltpu.VMEM((2, LANES), F32),
            pltpu.VMEM(tables.shape, BF16), pltpu.SMEM((2,), F32), pltpu.SMEM((2,), F32),
            pltpu.VMEM((8, 32, 256), BF16), pltpu.VMEM((8, 16, LANES), BF16), pltpu.VMEM((8, 16, LANES), F32), pltpu.VMEM((8, LANES), F32),
            pltpu.VMEM((8, 32, 256), BF16), pltpu.VMEM((8, 16, LANES), BF16), pltpu.VMEM((8, 16, LANES), F32), pltpu.VMEM((8, 8, LANES), F32),
            pltpu.VMEM((8, 16, LANES), F32), pltpu.VMEM((8, 16, LANES), F32),
            pltpu.VMEM((n_plane, 1, LANES), F32), pltpu.VMEM((n_column, 1, LANES), F32),
            pltpu.VMEM((1, LANES), F32), pltpu.VMEM((1, LANES), F32),
            pltpu.VMEM((4, LANES, LANES), F32), pltpu.VMEM((4, LANES, 256), F32), pltpu.VMEM((2, 4, 64, LANES), F32),
            pltpu.VMEM((2, 256, LANES), F32), pltpu.VMEM((4, LANES, LANES), F32), pltpu.VMEM((4, 64, 256), F32),
            pltpu.VMEM((2, 4, 64, LANES), F32),
            pltpu.VMEM((8, 4, 64, LANES), F32), pltpu.VMEM((8, 4, 64, LANES), F32),
            pltpu.VMEM((LANES, LANES), F32), pltpu.VMEM((LANES, LANES), F32),
            pltpu.VMEM((2, 4, 64, LANES), F32),
            dma((7,)), dma((5,)), dma((5,)), dma((2,)), dma((2,)),
        ],
        compiler_params=pltpu.CompilerParams(collective_id=0, has_side_effects=True),
    )(cotangent, amplitude, phase, position, profile, alt_weight, tables)
    return pl.pallas_call(
        functools.partial(finish, dims[0] * dims[1] * dims[2] * LANES),
        out_shape=(jax.ShapeDtypeStruct((LANES, LANES), F32), jax.ShapeDtypeStruct((2,), F32)),
        in_specs=[vmem, vmem],
        out_specs=(any_spec, smem),
        scratch_shapes=[pltpu.SemaphoreType.DMA],
    )(*(pltpu.with_memory_space_constraint(v, pltpu.VMEM) for v in (back, bins)))


def solution(mesh):
    dims = {32: (4, 2, 4), 2: (2, 1, 1)}[mesh.shape["sub"]]
    placed = (P("alt", "sub"), P("alt", "sub"), P("alt", "sub"), P(None, "sub"), P("alt"), P("alt"))
    return jax.shard_map(
        functools.partial(local, dims), mesh=mesh, in_specs=placed, out_specs=(P("alt", "sub"), P("alt")), check_vma=False
    )
```

```python
import functools

import jax
import jax.numpy as jnp
import numpy as np
from jax import lax
from jax.experimental import pallas as pl
from jax.experimental.pallas import tpu as pltpu
from jax.sharding import PartitionSpec as P

F32 = jnp.float32
BF16 = jnp.bfloat16
MESH = pl.DeviceIdType.MESH

N_PUPIL = 32
N_FIELD = 64
N_BINS = 16
N_ALT = 8
LANES = 128


def split_np(m):
    hi = np.asarray(m, np.float32).astype(BF16)
    lo = (np.asarray(m, np.float64) - hi.astype(np.float64)).astype(np.float32).astype(BF16)
    return hi, lo


def make_tables():
    n = np.arange(N_FIELD)
    angle = 2.0 * np.pi / N_FIELD * (np.outer(n, n) % N_FIELD)
    cos, sin = np.cos(angle), np.sin(angle)
    eye = np.eye(4)
    half_c, half_s = cos[:, :N_PUPIL], sin[:, :N_PUPIL]
    kc, ks = np.kron(eye, half_c), np.kron(eye, half_s)
    w1 = np.block([[kc.T, -ks.T], [ks.T, kc.T]])
    w3 = np.block([[kc, ks]])
    w4 = w3.T
    w5 = np.block([[kc, ks], [-ks, kc]])
    a2 = np.block([[half_c, half_s], [-half_s, half_c]])
    a3 = np.vstack([cos, sin])
    a5 = np.block([[cos[:N_PUPIL], -sin[:N_PUPIL]], [sin[:N_PUPIL], cos[:N_PUPIL]]])
    blocks = []
    for w in (w1[:, :256], w1[:, 256:], w3, w4, w5[:256], w5[256:]):
        blocks += list(split_np(w))
    for a in (a2, a3):
        hi, lo = split_np(a)
        blocks.append(np.concatenate([hi, hi, lo, np.zeros_like(lo)], axis=1))
    hi, lo = split_np(a5)
    blocks += [np.concatenate([hi, hi], axis=1), np.concatenate([lo, np.zeros_like(lo)], axis=1)]
    return np.concatenate(blocks, axis=0)


W1, W3, W4, W5 = (0, 512), 1024, 1536, (2048, 2560)
A2, A3, A5 = 3072, 3200, 3328


def split(x):
    hi = x.astype(BF16)
    return hi, (x - hi.astype(F32)).astype(BF16)


def mm(a, b):
    return jnp.dot(a, b, preferred_element_type=F32)


def lane_mm(parts, tab, row):
    rows = parts[0].shape[0]
    w_hi, w_lo = tab[row : row + 256, :], tab[row + 256 : row + 512, :]
    both = mm(jnp.concatenate(parts, axis=0), w_hi)
    return both[:rows] + both[rows:] + mm(parts[0], w_lo)


def row_mm(table, x):
    hi, lo = split(x)
    return mm(table, jnp.concatenate([hi, lo, hi], axis=0))


def sincos(x):
    n = jnp.floor(x * (2.0 / np.pi) + 0.5)
    r = x - n * 1.5703125
    r = r - n * 4.837512969970703125e-4
    r = r - n * 7.54978995489188216e-8
    z = r * r
    s = ((-1.9515295891e-4 * z + 8.3321608736e-3) * z - 1.6666654611e-1) * z * r + r
    c = ((2.443315711809948e-5 * z - 1.388731625493765e-3) * z + 4.166664568298827e-2) * z * z - 0.5 * z + 1.0
    q = n.astype(jnp.int32)
    odd = (q & 1) == 1
    sv = jnp.where(odd, c, s)
    cv = jnp.where(odd, s, c)
    sv = jnp.where((q & 2) == 2, -sv, sv)
    cv = jnp.where(((q + 1) & 2) == 2, -cv, cv)
    return sv, cv


def swap4(x):
    lane = lax.broadcasted_iota(jnp.int32, x[0].shape, 1)
    keep0 = ((lane // 4) % 2) == 0
    keep1 = ((lane // 8) % 2) == 0

    def pair(a, b, shift, keep):
        return (
            jnp.where(keep, a, pltpu.roll(b, shift, 1)),
            jnp.where(keep, pltpu.roll(a, LANES - shift, 1), b),
        )

    y0, y1 = pair(x[0], x[1], 4, keep0)
    y2, y3 = pair(x[2], x[3], 4, keep0)
    z0, z2 = pair(y0, y2, 8, keep1)
    z1, z3 = pair(y1, y3, 8, keep1)
    return z0, z1, z2, z3


def far_first(n):
    return sorted(range(n), key=lambda o: -min(o, n - o))


def kernel(
    dims,
    cot_hbm, amp_hbm, ph_hbm, pos_hbm, prof_hbm, wt_hbm,
    tab_hbm,
    grad_ref, bins_ref,
    cot_in, amp_in, ph_in, pos_ref,
    tab, prof_ref, wt_ref,
    cot_send, amp_send, ph_send, small_send,
    cot_recv, amp_recv, ph_recv, small_recv,
    back_send, back_recv, st_a, st_b, row_a, row_b,
    yu, uf, bw, yg, cs, gf, qf, ct, sn, er, ei, sf,
    load_sem, send_sem, recv_sem, sems_a, sems_b,
):
    ny, nz, nx = dims
    me = lax.axis_index("alt")
    sub = lax.axis_index("sub")
    y, zl, x = sub // (nz * nx), (sub // nx) % nz, sub % nx

    plane = []
    for oy in far_first(ny):
        for ox in far_first(nx):
            if oy or ox:
                qy, qx = (y + oy) % ny, (x + ox) % nx
                plane.append({"sub": qy * (nz * nx) + zl * nx + qx})
    column = []
    for oh in far_first(N_ALT // 2):
        for oz in range(nz):
            for oc in range(2):
                if oh or oz or oc:
                    qz, qa = (zl + oz) % nz, (me // 2 + oh) % (N_ALT // 2) * 2 + (me + oc) % 2
                    column.append({"sub": y * (nz * nx) + qz * nx + x, "alt": qa})
    my_plane = y * nx + x
    my_column = zl * N_ALT + me

    loads = []
    for src, dst in (
        (ph_hbm, ph_in), (amp_hbm, amp_in), (cot_hbm, cot_in), (pos_hbm, pos_ref),
        (prof_hbm, prof_ref), (wt_hbm, wt_ref), (tab_hbm, tab),
    ):
        loads.append(pltpu.make_async_copy(src, dst, load_sem.at[len(loads)]))
    loads[0].start()
    loads[1].start()

    barrier = pltpu.get_barrier_semaphore()
    for device in column + plane:
        pl.semaphore_signal(barrier, inc=1, device_id=device, device_id_type=MESH)

    for cp in loads[2:]:
        cp.start()

    loads[0].wait()
    t = jnp.concatenate(swap4([ph_in[32 * k : 32 * k + 32, :] for k in range(4)]), axis=0).T
    ph_send[...] = t.reshape(8, 16, LANES)
    loads[1].wait()
    amp = amp_in[...].astype(F32)
    t = jnp.concatenate(swap4([amp[32 * k : 32 * k + 32, :] for k in range(4)]), axis=0).T
    amp_send[...] = t.reshape(8, 16, LANES).astype(BF16)

    loads[4].wait()
    loads[5].wait()
    row = lax.broadcasted_iota(jnp.int32, (8, LANES), 0)
    lane = lax.broadcasted_iota(jnp.int32, (8, LANES), 1)
    small = jnp.zeros((1, LANES), F32)
    for b in range(2):
        small = jnp.where(lane[:1] == 2 * me + b, prof_ref[b], small)
        small = jnp.where(lane[:1] == N_BINS + 2 * me + b, wt_ref[b], small)
    small_send[...] = small

    pl.semaphore_wait(barrier, len(plane) + len(column))

    order = [(2, 0), (2, 1), (1, 0), (3, 0), (1, 1), (3, 1), (0, 1)]
    kinds = ((small_send, small_recv), (ph_send, ph_recv), (amp_send, amp_recv), (cot_send, cot_recv), (back_send, back_recv))

    def peer_of(offset):
        return (me // 2 + offset[0]) % (N_ALT // 2) * 2 + (me + offset[1]) % 2

    def exchange(kind, offset):
        src, dst = kinds[kind]
        peer = peer_of(offset)
        return pltpu.make_async_remote_copy(
            src_ref=src if kind == 0 else src.at[peer],
            dst_ref=dst.at[me],
            send_sem=send_sem.at[kind],
            recv_sem=recv_sem.at[kind],
            device_id={"alt": peer},
            device_id_type=MESH,
        )

    def start(kind):
        for offset in order:
            exchange(kind, offset).start()

    def wait_in(kind):
        dst = kinds[kind][1].at[pl.ds(0, N_ALT - 1)]
        pltpu.make_async_copy(dst, dst, recv_sem.at[kind]).wait()

    def wait_out(kind):
        dst = kinds[kind][1].at[pl.ds(0, N_ALT - 1)]
        pltpu.make_async_copy(dst, dst, send_sem.at[kind]).wait()

    start(0)
    start(1)
    start(2)

    loads[2].wait()
    for half in range(2):
        z = swap4([cot_in[256 * half + 64 * k : 256 * half + 64 * k + 64, :].astype(F32) for k in range(4)])
        for u in range(2):
            t = jnp.concatenate([z[2 * u], z[2 * u + 1]], axis=0).T
            cot_send[:, 16 * half : 16 * half + 16, LANES * u : LANES * u + LANES] = t.reshape(8, 16, LANES).astype(BF16)
    start(3)

    small_recv[me] = small
    ph_recv[me] = ph_send[me]
    amp_recv[me] = amp_send[me]
    cot_recv[me] = cot_send[me]

    src = lax.broadcasted_iota(jnp.int32, (LANES, 4 * LANES), 0)
    dst = lax.broadcasted_iota(jnp.int32, (LANES, 4 * LANES), 1)
    pick = (src == 16 * me + 4 * ((dst % LANES) // 32) + dst // LANES).astype(F32)
    loads[3].wait()
    pos = jnp.concatenate([pos_ref[...], jnp.zeros((6, LANES), F32)], axis=0)
    pos = jnp.dot(pos, pick, precision=lax.Precision.HIGHEST, preferred_element_type=F32)
    r64 = lax.broadcasted_iota(jnp.int32, (N_FIELD, LANES), 0)
    l64 = lax.broadcasted_iota(jnp.int32, (N_FIELD, LANES), 1)
    dr = jnp.where(r64 < 32, r64, r64 - N_FIELD).astype(F32)
    dc = (l64 % 32).astype(F32)
    twice = jnp.where(l64 % 32 == 0, 1.0, 2.0).astype(F32)
    for g in range(4):
        px = pos[0:1, LANES * g : LANES * g + LANES]
        py = pos[1:2, LANES * g : LANES * g + LANES]
        s, c = sincos(0.05 * (px * dc + py * dr))
        c2, s2 = c * c - s * s, 2.0 * s * c
        for j in range(8):
            ct[j, g], sn[j, g] = c, s
            if j < 7:
                c, s = c * c2 - s * s2, s * c2 + c * s2

    wait_in(0)
    bins = small_recv[0]
    for k in range(1, N_ALT):
        bins = bins + small_recv[k]
    prof = jnp.where(lane[:1] < N_BINS, bins, 0.0)
    wt = jnp.where(lane[:1] < N_BINS, pltpu.roll(bins, LANES - N_BINS, 1), 0.0)
    total = jnp.sum(prof, axis=1, keepdims=True)
    omega = prof * wt / total
    for g in range(4):
        re = jnp.zeros((N_FIELD, LANES), F32)
        im = jnp.zeros((N_FIELD, LANES), F32)
        for j in range(8):
            up, down = omega[:, 8 + j : 9 + j], omega[:, 7 - j : 8 - j]
            re = re + (up + down) * ct[j, g]
            im = im - (up - down) * sn[j, g]
        sf[0, g] = re * twice
        sf[1, g] = im * twice

    loads[6].wait()
    wait_in(1)
    wait_in(2)
    s, c = sincos(ph_recv[...].reshape(LANES, LANES))
    amp = amp_recv[...].astype(F32).reshape(LANES, LANES)
    e_re, e_im = amp * c, amp * s
    er[...] = e_re
    ei[...] = e_im
    e_both = split(jnp.concatenate([e_re, e_im], axis=1))
    for h in range(2):
        half = lane_mm(e_both, tab, W1[h])
        yu[2 * h], yu[2 * h + 1] = half[:, :LANES], half[:, LANES:]
    a2, a3 = tab[A2 : A2 + LANES, :192], tab[A3 : A3 + LANES, :192]
    power = []
    for g in range(4):
        m = [yu.at[k][pl.ds(g, 32, stride=4), :] for k in range(4)]
        m = [jnp.concatenate([m[0], m[1]], axis=1), jnp.concatenate([m[2], m[3]], axis=1)]
        u = row_mm(a2, jnp.concatenate(m, axis=0))
        uf[g] = u
        power.append(u[:64] * u[:64] + u[64:] * u[64:])
    yb = lane_mm(split(jnp.concatenate(power, axis=0)), tab, W3)
    keep = jnp.where(r64 == 32, 0.0, twice) * (1.0 / (1024.0 * 4096.0))
    for g in range(4):
        v = row_mm(a3, yb[64 * g : 64 * g + 64, :])
        bw[0, g] = (v[:64, :LANES] - v[64:, LANES:]) * keep
        bw[1, g] = (v[:64, LANES:] + v[64:, :LANES]) * keep

    wait_in(3)
    cot = cot_recv[...].reshape(256, 256)
    yy = mm(cot, tab[W3 : W3 + 256, :]) + mm(cot, tab[W3 + 256 : W3 + 512, :])
    yg[0], yg[1] = yy[:, :LANES], yy[:, LANES:]
    for g in range(4):
        m = [yg.at[k][pl.ds(g, 64, stride=4), :] for k in range(2)]
        v = row_mm(a3, jnp.concatenate(m, axis=1))
        g_re = v[:64, :LANES] - v[64:, LANES:]
        g_im = v[:64, LANES:] + v[64:, :LANES]
        b_re, b_im = bw[0, g], bw[1, g]
        qf[0, g] = g_re * b_re + g_im * b_im
        qf[1, g] = g_im * b_re - g_re * b_im
        gf[g] = jnp.concatenate([g_re, g_im], axis=1)

    sums = []
    for part, table in ((0, ct), (1, sn)):
        rows = []
        for j in range(8):
            acc = jnp.zeros((8, LANES), F32)
            for g in range(4):
                acc = acc + jnp.sum((qf[part, g] * table[j, g]).reshape(8, 8, LANES), axis=0)
            rows.append(jnp.sum(acc, axis=0, keepdims=True))
        sums.append(jnp.sum(jnp.concatenate(rows, axis=0), axis=1, keepdims=True))
    here = jnp.where(lane == 8 + row, sums[0] + sums[1], 0.0) + jnp.where(lane == 7 - row, sums[0] - sums[1], 0.0)
    mine = jnp.sum(here, axis=0, keepdims=True)
    row_a[...] = mine
    st_a[my_column] = mine

    def post(peers, me_slot, src, dst, sems):
        for device in peers:
            pltpu.make_async_remote_copy(
                src_ref=src, dst_ref=dst.at[me_slot], send_sem=sems.at[0], recv_sem=sems.at[1],
                device_id=device, device_id_type=MESH,
            ).start()

    def wait_all(peers, dst, sem):
        if peers:
            part = dst.at[pl.ds(0, len(peers))]
            pltpu.make_async_copy(part, part, sem).wait()

    post(column, my_column, row_a, st_a, sems_a)

    z = []
    for g in range(4):
        g_re, g_im, s_re, s_im = gf[g, :, :LANES], gf[g, :, LANES:], sf[0, g], sf[1, g]
        v = row_mm(a3, jnp.concatenate([g_re * s_re - g_im * s_im, g_re * s_im + g_im * s_re], axis=1))
        z.append(jnp.concatenate([v[:64, :LANES] + v[64:, LANES:], v[:64, LANES:] - v[64:, :LANES]], axis=1))
    g_hat = lane_mm(split(jnp.concatenate(z, axis=0)), tab, W4)
    for g in range(4):
        gh = g_hat[64 * g : 64 * g + 64, :]
        v = jnp.concatenate([uf[g, :64, :] * gh, uf[g, 64:, :] * gh], axis=0)
        hi, lo = split(v)
        v = mm(tab[A5 : A5 + 64, :], jnp.concatenate([hi, lo], axis=0)) + mm(tab[A5 + 64 : A5 + 128, :LANES], hi)
        for k in range(2):
            cs.at[k][pl.ds(g, 32, stride=4), :] = v[:32, LANES * k : LANES * k + LANES]
            cs.at[2 + k][pl.ds(g, 32, stride=4), :] = v[32:, LANES * k : LANES * k + LANES]
    conv = sum(lane_mm(split(jnp.concatenate([cs[2 * h], cs[2 * h + 1]], axis=1)), tab, W5[h]) for h in range(2))
    grad = (er[...] * conv[:, LANES:] - ei[...] * conv[:, :LANES]) * (2.0 / (1024.0 * 4096.0))
    back_send[...] = grad.reshape(8, 16, LANES)
    start(4)
    back_recv[me] = back_send[me]

    wait_all(column, st_a, sems_a.at[1])
    acc = st_a[0]
    for k in range(1, nz * N_ALT):
        acc = acc + st_a[k]
    row_b[...] = acc
    st_b[my_plane] = acc
    post(plane, my_plane, row_b, st_b, sems_b)

    wait_in(4)
    m = back_recv[...].reshape(LANES, LANES).T
    rows = swap4([m[32 * k : 32 * k + 32, :] for k in range(4)])
    for k in range(4):
        grad_ref[32 * k : 32 * k + 32, :] = rows[k]

    wait_all(plane, st_b, sems_b.at[1])
    stat = st_b[0]
    for k in range(1, ny * nx):
        stat = stat + st_b[k]
    centre = jnp.sum(prof * wt * stat, axis=1, keepdims=True)
    pg = (wt * stat / total - centre / (total * total)) * (1.0 / (ny * nz * nx * LANES))
    own = [jnp.sum(jnp.where(lane[:1] == 2 * me + b, pg, 0.0), axis=1, keepdims=True) for b in range(2)]
    bins_ref[...] = jnp.where(lane[:1] == 0, own[0], own[1])

    for kind in range(5):
        wait_out(kind)
    wait_all(column, st_a, sems_a.at[0])
    wait_all(plane, st_b, sems_b.at[0])


def finish(grad_ref, bins_ref, out_hbm, pg_hbm, pg_ref, sems):
    copies = [pltpu.make_async_copy(grad_ref, out_hbm, sems.at[0]), pltpu.make_async_copy(pg_ref, pg_hbm, sems.at[1])]
    copies[0].start()
    pg_ref[0] = bins_ref[0, 0]
    pg_ref[1] = bins_ref[0, 1]
    copies[1].start()
    for cp in copies:
        cp.wait()


def local(dims, cotangent, amplitude, phase, position, profile, alt_weight):
    tables = jnp.asarray(make_tables())
    any_spec = pl.BlockSpec(memory_space=pl.ANY)
    vmem = pl.BlockSpec(memory_space=pltpu.VMEM)
    n_plane, n_column = dims[0] * dims[2], dims[1] * N_ALT
    dma = pltpu.SemaphoreType.DMA
    back, bins = pl.pallas_call(
        functools.partial(kernel, dims),
        out_shape=(pltpu.VMEM((LANES, LANES), F32), pltpu.VMEM((1, LANES), F32)),
        in_specs=[any_spec] * 7,
        out_specs=(vmem, vmem),
        scratch_shapes=[
            pltpu.VMEM((512, LANES), BF16), pltpu.VMEM((LANES, LANES), BF16), pltpu.VMEM((LANES, LANES), F32), pltpu.VMEM((2, LANES), F32),
            pltpu.VMEM(tables.shape, BF16), pltpu.SMEM((2,), F32), pltpu.SMEM((2,), F32),
            pltpu.VMEM((8, 32, 256), BF16), pltpu.VMEM((8, 16, LANES), BF16), pltpu.VMEM((8, 16, LANES), F32), pltpu.VMEM((1, LANES), F32),
            pltpu.VMEM((8, 32, 256), BF16), pltpu.VMEM((8, 16, LANES), BF16), pltpu.VMEM((8, 16, LANES), F32), pltpu.VMEM((8, 1, LANES), F32),
            pltpu.VMEM((8, 16, LANES), F32), pltpu.VMEM((8, 16, LANES), F32),
            pltpu.VMEM((n_column, 1, LANES), F32), pltpu.VMEM((n_plane, 1, LANES), F32),
            pltpu.VMEM((1, LANES), F32), pltpu.VMEM((1, LANES), F32),
            pltpu.VMEM((4, LANES, LANES), F32), pltpu.VMEM((4, LANES, 256), F32), pltpu.VMEM((2, 4, 64, LANES), F32),
            pltpu.VMEM((2, 256, LANES), F32), pltpu.VMEM((4, LANES, LANES), F32), pltpu.VMEM((4, 64, 256), F32),
            pltpu.VMEM((2, 4, 64, LANES), F32),
            pltpu.VMEM((8, 4, 64, LANES), F32), pltpu.VMEM((8, 4, 64, LANES), F32),
            pltpu.VMEM((LANES, LANES), F32), pltpu.VMEM((LANES, LANES), F32),
            pltpu.VMEM((2, 4, 64, LANES), F32),
            dma((7,)), dma((5,)), dma((5,)), dma((2,)), dma((2,)),
        ],
        compiler_params=pltpu.CompilerParams(collective_id=0, has_side_effects=True),
    )(cotangent, amplitude, phase, position, profile, alt_weight, tables)
    return pl.pallas_call(
        finish,
        out_shape=(jax.ShapeDtypeStruct((LANES, LANES), F32), jax.ShapeDtypeStruct((2,), F32)),
        in_specs=[vmem, vmem],
        out_specs=(any_spec, any_spec),
        scratch_shapes=[pltpu.SMEM((2,), F32), dma((2,))],
    )(*(pltpu.with_memory_space_constraint(v, pltpu.VMEM) for v in (back, bins)))


def solution(mesh):
    dims = {32: (4, 2, 4), 2: (2, 1, 1)}[mesh.shape["sub"]]
    placed = (P("alt", "sub"), P("alt", "sub"), P("alt", "sub"), P(None, "sub"), P("alt"), P("alt"))
    return jax.shard_map(
        functools.partial(local, dims), mesh=mesh, in_specs=placed, out_specs=(P("alt", "sub"), P("alt")), check_vma=False
    )
```

```python
import functools

import jax
import jax.numpy as jnp
import numpy as np
from jax import lax
from jax.experimental import pallas as pl
from jax.experimental.pallas import tpu as pltpu
from jax.sharding import PartitionSpec as P

F32 = jnp.float32
BF16 = jnp.bfloat16
MESH = pl.DeviceIdType.MESH

N_PUPIL = 32
N_FIELD = 64
N_BINS = 16
N_ALT = 8
LANES = 128


def split_np(m):
    hi = np.asarray(m, np.float32).astype(BF16)
    lo = (np.asarray(m, np.float64) - hi.astype(np.float64)).astype(np.float32).astype(BF16)
    return hi, lo


def make_tables():
    n = np.arange(N_FIELD)
    angle = 2.0 * np.pi / N_FIELD * (np.outer(n, n) % N_FIELD)
    cos, sin = np.cos(angle), np.sin(angle)
    eye = np.eye(4)
    half_c, half_s = cos[:, :N_PUPIL], sin[:, :N_PUPIL]
    kc, ks = np.kron(eye, half_c), np.kron(eye, half_s)
    w1 = np.block([[kc.T, -ks.T], [ks.T, kc.T]])
    w3 = np.block([[kc, ks]])
    w4 = w3.T
    w5 = np.block([[kc, ks], [-ks, kc]])
    a2 = np.block([[half_c, half_s], [-half_s, half_c]])
    a3 = np.vstack([half_c.T, half_s.T])
    a4 = np.block([[half_c, 0 * half_c], [0 * half_s, half_s]])
    a5 = np.block([[cos[:N_PUPIL], -sin[:N_PUPIL]], [sin[:N_PUPIL], cos[:N_PUPIL]]])
    blocks = []
    for w in (w1[:, :256], w1[:, 256:], w3, w4, w5[:256], w5[256:]):
        blocks += list(split_np(w))
    for a in (a2, a4, a3):
        hi, lo = split_np(a)
        blocks.append(np.concatenate([hi, hi, lo, np.zeros_like(lo)], axis=1))
    hi, lo = split_np(a5)
    blocks += [np.concatenate([hi, hi], axis=1), np.concatenate([lo, np.zeros_like(lo)], axis=1)]
    return np.concatenate(blocks, axis=0)


W1, W3, W4, W5 = (0, 512), 1024, 1536, (2048, 2560)
A2, A4, A3, A5 = 3072, 3200, 3328, 3392


def split(x):
    hi = x.astype(BF16)
    return hi, (x - hi.astype(F32)).astype(BF16)


def mm(a, b):
    return jnp.dot(a, b, preferred_element_type=F32)


def lane_mm(parts, tab, row):
    rows = parts[0].shape[0]
    w_hi, w_lo = tab[row : row + 256, :], tab[row + 256 : row + 512, :]
    both = mm(jnp.concatenate(parts, axis=0), w_hi)
    return both[:rows] + both[rows:] + mm(parts[0], w_lo)


def row_mm(table, x):
    hi, lo = split(x)
    return mm(table, jnp.concatenate([hi, lo, hi], axis=0))


def both_signs(v):
    c_re, c_im, s_re, s_im = v[:32, :LANES], v[:32, LANES:], v[32:, :LANES], v[32:, LANES:]
    return jnp.concatenate([c_re - s_im, c_re + s_im], axis=0), jnp.concatenate([c_im + s_re, c_im - s_re], axis=0)


def sincos(x):
    n = jnp.floor(x * (2.0 / np.pi) + 0.5)
    r = x - n * 1.5703125
    r = r - n * 4.837512969970703125e-4
    r = r - n * 7.54978995489188216e-8
    z = r * r
    s = ((-1.9515295891e-4 * z + 8.3321608736e-3) * z - 1.6666654611e-1) * z * r + r
    c = ((2.443315711809948e-5 * z - 1.388731625493765e-3) * z + 4.166664568298827e-2) * z * z - 0.5 * z + 1.0
    q = n.astype(jnp.int32)
    odd = (q & 1) == 1
    sv = jnp.where(odd, c, s)
    cv = jnp.where(odd, s, c)
    sv = jnp.where((q & 2) == 2, -sv, sv)
    cv = jnp.where(((q + 1) & 2) == 2, -cv, cv)
    return sv, cv


def swap4(x):
    lane = lax.broadcasted_iota(jnp.int32, x[0].shape, 1)
    keep0 = ((lane // 4) % 2) == 0
    keep1 = ((lane // 8) % 2) == 0

    def pair(a, b, shift, keep):
        return (
            jnp.where(keep, a, pltpu.roll(b, shift, 1)),
            jnp.where(keep, pltpu.roll(a, LANES - shift, 1), b),
        )

    y0, y1 = pair(x[0], x[1], 4, keep0)
    y2, y3 = pair(x[2], x[3], 4, keep0)
    z0, z2 = pair(y0, y2, 8, keep1)
    z1, z3 = pair(y1, y3, 8, keep1)
    return z0, z1, z2, z3


def far_first(n):
    return sorted(range(n), key=lambda o: -min(o, n - o))


def kernel(
    dims,
    cot_hbm, amp_hbm, ph_hbm, pos_hbm, prof_hbm, wt_hbm,
    tab_hbm,
    grad_ref, bins_ref,
    cot_in, amp_in, ph_in, pos_ref,
    tab, prof_ref, wt_ref,
    cot_send, amp_send, ph_send, small_send,
    cot_recv, amp_recv, ph_recv, small_recv,
    back_send, back_recv, st_a, st_b, row_a, row_b,
    yu, uf, bw, yg, cs, gf, yt, xt, ct, sn, er, ei, sf,
    load_sem, send_sem, recv_sem, sems_a, sems_b,
):
    ny, nz, nx = dims
    me = lax.axis_index("alt")
    sub = lax.axis_index("sub")
    x, yz = lax.rem(sub, nx), lax.div(sub, nx)
    y, zl = lax.div(yz, nz), lax.rem(yz, nz)
    core, high = lax.rem(me, 2), lax.div(me, 2)
    nh = N_ALT // 2
    at_high = [2 * lax.rem(high + o, nh) for o in range(nh)]
    at_core = [core, 1 - core]

    at_y = [lax.rem(y + o, ny) * (nz * nx) + zl * nx for o in range(ny)]
    at_x = [lax.rem(x + o, nx) for o in range(nx)]
    plane = [{"sub": at_y[oy] + at_x[ox]} for oy in far_first(ny) for ox in far_first(nx) if oy or ox]
    at_z = [y * (nz * nx) + lax.rem(zl + o, nz) * nx + x for o in range(nz)]
    column = [
        {"sub": at_z[oz], "alt": at_high[oh] + at_core[oc]}
        for oh in far_first(nh)
        for oz in range(nz)
        for oc in range(2)
        if oh or oz or oc
    ]
    my_plane = y * nx + x
    my_column = zl * N_ALT + me

    loads = []
    for src, dst in (
        (ph_hbm, ph_in), (amp_hbm, amp_in), (cot_hbm, cot_in), (pos_hbm, pos_ref),
        (prof_hbm, prof_ref), (wt_hbm, wt_ref), (tab_hbm, tab),
    ):
        loads.append(pltpu.make_async_copy(src, dst, load_sem.at[len(loads)]))
    for k in range(4):
        part = pl.ds(32 * k, 32)
        pltpu.make_async_copy(ph_hbm.at[part], ph_in.at[part], load_sem.at[0]).start()
    loads[1].start()

    barrier = pltpu.get_barrier_semaphore()
    for device in column + plane:
        pl.semaphore_signal(barrier, inc=1, device_id=device, device_id_type=MESH)

    for cp in loads[2:]:
        cp.start()

    loads[0].wait()
    t = jnp.concatenate(swap4([ph_in[32 * k : 32 * k + 32, :] for k in range(4)]), axis=0).T
    ph_send[...] = t.reshape(8, 16, LANES)
    loads[1].wait()
    amp = amp_in[...].astype(F32)
    t = jnp.concatenate(swap4([amp[32 * k : 32 * k + 32, :] for k in range(4)]), axis=0).T
    amp_send[...] = t.reshape(8, 16, LANES).astype(BF16)

    loads[2].wait()
    for half in range(2):
        z = swap4([cot_in[256 * half + 64 * k : 256 * half + 64 * k + 64, :].astype(F32) for k in range(4)])
        for u in range(2):
            t = jnp.concatenate([z[2 * u], z[2 * u + 1]], axis=0).T
            cot_send[:, 16 * half : 16 * half + 16, LANES * u : LANES * u + LANES] = t.reshape(8, 16, LANES).astype(BF16)
    loads[4].wait()
    loads[5].wait()
    row = lax.broadcasted_iota(jnp.int32, (8, LANES), 0)
    lane = lax.broadcasted_iota(jnp.int32, (8, LANES), 1)
    small = jnp.zeros((1, LANES), F32)
    for b in range(2):
        small = jnp.where(lane[:1] == 2 * me + b, prof_ref[b], small)
        small = jnp.where(lane[:1] == N_BINS + 2 * me + b, wt_ref[b], small)
    small_send[...] = small

    pl.semaphore_wait(barrier, len(plane) + len(column))

    order = [(2, 0), (2, 1), (1, 0), (3, 0), (1, 1), (3, 1), (0, 1)]
    kinds = ((small_send, small_recv), (ph_send, ph_recv), (amp_send, amp_recv), (cot_send, cot_recv), (back_send, back_recv))

    def peer_of(offset):
        return at_high[offset[0]] + at_core[offset[1]]

    def exchange(kind, offset):
        src, dst = kinds[kind]
        peer = peer_of(offset)
        return pltpu.make_async_remote_copy(
            src_ref=src if kind == 0 else src.at[peer],
            dst_ref=dst.at[me],
            send_sem=send_sem.at[kind],
            recv_sem=recv_sem.at[kind],
            device_id={"alt": peer},
            device_id_type=MESH,
        )

    def start(kind):
        for offset in order:
            exchange(kind, offset).start()

    def wait_in(kind):
        dst = kinds[kind][1].at[pl.ds(0, N_ALT - 1)]
        pltpu.make_async_copy(dst, dst, recv_sem.at[kind]).wait()

    def wait_out(kind):
        dst = kinds[kind][1].at[pl.ds(0, N_ALT - 1)]
        pltpu.make_async_copy(dst, dst, send_sem.at[kind]).wait()

    start(0)
    start(1)
    start(2)
    start(3)

    small_recv[me] = small
    ph_recv[me] = ph_send[me]
    amp_recv[me] = amp_send[me]
    cot_recv[me] = cot_send[me]

    src = lax.broadcasted_iota(jnp.int32, (LANES, 4 * LANES), 0)
    dst = lax.broadcasted_iota(jnp.int32, (LANES, 4 * LANES), 1)
    pick = (src == 16 * me + 4 * ((dst % LANES) // 32) + dst // LANES).astype(F32)
    loads[3].wait()
    pos = jnp.concatenate([pos_ref[...], jnp.zeros((6, LANES), F32)], axis=0)
    pos = jnp.dot(pos, pick, precision=lax.Precision.HIGHEST, preferred_element_type=F32)
    r64 = lax.broadcasted_iota(jnp.int32, (N_FIELD, LANES), 0)
    l64 = lax.broadcasted_iota(jnp.int32, (N_FIELD, LANES), 1)
    dr = jnp.where(r64 < 32, r64, 32 - r64).astype(F32)
    dc = (l64 % 32).astype(F32)
    twice = jnp.where(r64 == 32, 0.0, jnp.where(l64 % 32 == 0, 1.0, 2.0)).astype(F32)
    for g in range(4):
        px = pos[0:1, LANES * g : LANES * g + LANES]
        py = pos[1:2, LANES * g : LANES * g + LANES]
        s, c = sincos(0.05 * (px * dc + py * dr))
        c2, s2 = c * c - s * s, 2.0 * s * c
        for j in range(8):
            ct[j, g], sn[j, g] = c, s
            if j < 7:
                c, s = c * c2 - s * s2, s * c2 + c * s2

    r32 = lax.broadcasted_iota(jnp.int32, (32, LANES), 0)
    l32 = lax.broadcasted_iota(jnp.int32, (32, LANES), 1)
    step = 0.05 * (2 * (r32 % 8) + 1).astype(F32)
    at = l32 % 64
    dr_lane = jnp.where(at < 32, at, 32 - at).astype(F32)
    for g in range(4):
        here = l32 == 16 * me + 4 * (r32 // 8) + g
        y_row = jnp.sum(jnp.where(here, pos_ref[1:2, :], 0.0), axis=1, keepdims=True)
        s, c = sincos(step * y_row * dr_lane)
        hi, lo = split(jnp.concatenate([c, s], axis=0))
        yt[g, :, :LANES], yt[g, :, LANES:] = hi, lo
        s, c = sincos(step * pos[0:1, LANES * g : LANES * g + LANES] * (l32 % 32).astype(F32))
        own = r32 // 8 == l32 // 32
        xt[g, 0], xt[g, 1] = jnp.where(own, c, 0.0), jnp.where(own, s, 0.0)

    wait_in(0)
    bins = small_recv[0]
    for k in range(1, N_ALT):
        bins = bins + small_recv[k]
    prof = jnp.where(lane[:1] < N_BINS, bins, 0.0)
    wt = jnp.where(lane[:1] < N_BINS, pltpu.roll(bins, LANES - N_BINS, 1), 0.0)
    total = jnp.sum(prof, axis=1, keepdims=True)
    omega = prof * wt / total
    for g in range(4):
        re = jnp.zeros((N_FIELD, LANES), F32)
        im = jnp.zeros((N_FIELD, LANES), F32)
        for j in range(8):
            up, down = omega[:, 8 + j : 9 + j], omega[:, 7 - j : 8 - j]
            re = re + (up + down) * ct[j, g]
            im = im - (up - down) * sn[j, g]
        sf[0, g] = re * twice
        sf[1, g] = im * twice

    loads[6].wait()
    wait_in(1)
    s, c = sincos(ph_recv[...].reshape(LANES, LANES))
    er[...], ei[...] = c, s
    wait_in(2)
    c, s = er[...], ei[...]
    amp = amp_recv[...].astype(F32).reshape(LANES, LANES)
    e_re, e_im = amp * c, amp * s
    er[...] = e_re
    ei[...] = e_im
    e_both = split(jnp.concatenate([e_re, e_im], axis=1))
    for h in range(2):
        half = lane_mm(e_both, tab, W1[h])
        yu[2 * h], yu[2 * h + 1] = half[:, :LANES], half[:, LANES:]
    a2, a3 = tab[A2 : A2 + LANES, :192], tab[A3 : A3 + 64, :192]
    power = []
    for g in range(4):
        m = [yu.at[k][pl.ds(g, 32, stride=4), :] for k in range(4)]
        m = [jnp.concatenate([m[0], m[1]], axis=1), jnp.concatenate([m[2], m[3]], axis=1)]
        u = row_mm(a2, jnp.concatenate(m, axis=0))
        uf[g] = u
        power.append(u[:64] * u[:64] + u[64:] * u[64:])
    yb = lane_mm(split(jnp.concatenate(power, axis=0)), tab, W3)
    keep = twice * (1.0 / (1024.0 * 4096.0))
    for g in range(4):
        v = row_mm(a3, yb[64 * g : 64 * g + 64, :])
        b_re, b_im = both_signs(v)
        bw[0, g], bw[1, g] = b_re * keep, b_im * keep

    wait_in(3)
    cot = cot_recv[...].reshape(256, 256)
    parts = []
    yy = mm(cot, tab[W3 : W3 + 256, :]) + mm(cot, tab[W3 + 256 : W3 + 512, :])
    yg[0], yg[1] = yy[:, :LANES], yy[:, LANES:]
    for g in range(4):
        m = [yg.at[k][pl.ds(g, 64, stride=4), :] for k in range(2)]
        v = row_mm(a3, jnp.concatenate(m, axis=1))
        g_re, g_im = both_signs(v)
        b_re, b_im = bw[0, g], bw[1, g]
        hi, lo = split(jnp.concatenate([g_re * b_re + g_im * b_im, g_im * b_re - g_re * b_im], axis=1))
        m = mm(yt[g], jnp.concatenate([hi, lo, hi, lo], axis=0))
        parts.append((
            xt[g, 0] * m[:32, :LANES] - xt[g, 1] * m[32:, :LANES],
            xt[g, 1] * m[:32, LANES:] + xt[g, 0] * m[32:, LANES:],
        ))
        gf[g] = jnp.concatenate([g_re, g_im], axis=1)

    sums = []
    for k in range(2):
        acc = parts[0][k] + parts[1][k] + parts[2][k] + parts[3][k]
        acc = acc[:8] + acc[8:16] + acc[16:24] + acc[24:]
        sums.append(jnp.sum(acc, axis=1, keepdims=True))
    here = jnp.where(lane == 8 + row, sums[0] + sums[1], 0.0) + jnp.where(lane == 7 - row, sums[0] - sums[1], 0.0)
    mine = jnp.sum(here, axis=0, keepdims=True)
    row_a[...] = mine
    st_a[my_column] = mine

    def post(peers, me_slot, src, dst, sems):
        for device in peers:
            pltpu.make_async_remote_copy(
                src_ref=src, dst_ref=dst.at[me_slot], send_sem=sems.at[0], recv_sem=sems.at[1],
                device_id=device, device_id_type=MESH,
            ).start()

    def wait_all(peers, dst, sem):
        if peers:
            part = dst.at[pl.ds(0, len(peers))]
            pltpu.make_async_copy(part, part, sem).wait()

    post(column, my_column, row_a, st_a, sems_a)

    @pl.when(me >= 0)
    def _():
        z = []
        for g in range(4):
            g_re, g_im, s_re, s_im = gf[g, :, :LANES], gf[g, :, LANES:], sf[0, g], sf[1, g]
            v = jnp.concatenate([g_re * s_re - g_im * s_im, g_re * s_im + g_im * s_re], axis=1)
            v = row_mm(tab[A4 : A4 + LANES, :192], jnp.concatenate([v[:32] + v[32:], v[:32] - v[32:]], axis=0))
            z.append(jnp.concatenate([v[:64, :LANES] + v[64:, LANES:], v[:64, LANES:] - v[64:, :LANES]], axis=1))
        g_hat = lane_mm(split(jnp.concatenate(z, axis=0)), tab, W4)
        for g in range(4):
            gh = g_hat[64 * g : 64 * g + 64, :]
            v = jnp.concatenate([uf[g, :64, :] * gh, uf[g, 64:, :] * gh], axis=0)
            hi, lo = split(v)
            v = mm(tab[A5 : A5 + 64, :], jnp.concatenate([hi, lo], axis=0)) + mm(tab[A5 + 64 : A5 + 128, :LANES], hi)
            for k in range(2):
                cs.at[k][pl.ds(g, 32, stride=4), :] = v[:32, LANES * k : LANES * k + LANES]
                cs.at[2 + k][pl.ds(g, 32, stride=4), :] = v[32:, LANES * k : LANES * k + LANES]
        conv = sum(lane_mm(split(jnp.concatenate([cs[2 * h], cs[2 * h + 1]], axis=1)), tab, W5[h]) for h in range(2))
        grad = (er[...] * conv[:, LANES:] - ei[...] * conv[:, :LANES]) * (2.0 / (1024.0 * 4096.0))
        back_send[...] = grad.reshape(8, 16, LANES)
    start(4)
    back_recv[me] = back_send[me]

    wait_all(column, st_a, sems_a.at[1])
    acc = st_a[0]
    for k in range(1, nz * N_ALT):
        acc = acc + st_a[k]
    row_b[...] = acc
    st_b[my_plane] = acc
    post(plane, my_plane, row_b, st_b, sems_b)

    wait_in(4)
    m = back_recv[...].reshape(LANES, LANES).T
    rows = swap4([m[32 * k : 32 * k + 32, :] for k in range(4)])
    for k in range(4):
        grad_ref[32 * k : 32 * k + 32, :] = rows[k]

    wait_all(plane, st_b, sems_b.at[1])
    stat = st_b[0]
    for k in range(1, ny * nx):
        stat = stat + st_b[k]
    centre = jnp.sum(prof * wt * stat, axis=1, keepdims=True)
    pg = (wt * stat / total - centre / (total * total)) * (1.0 / (ny * nz * nx * LANES))
    own = [jnp.sum(jnp.where(lane[:1] == 2 * me + b, pg, 0.0), axis=1, keepdims=True) for b in range(2)]
    bins_ref[...] = jnp.where(lane[:1] == 0, own[0], own[1])

    for kind in range(5):
        wait_out(kind)
    wait_all(column, st_a, sems_a.at[0])
    wait_all(plane, st_b, sems_b.at[0])


def finish(grad_ref, bins_ref, out_hbm, pg_hbm, pg_ref, sems):
    copies = [pltpu.make_async_copy(grad_ref, out_hbm, sems.at[0]), pltpu.make_async_copy(pg_ref, pg_hbm, sems.at[1])]
    for k in range(4):
        part = pl.ds(32 * k, 32)
        pltpu.make_async_copy(grad_ref.at[part], out_hbm.at[part], sems.at[0]).start()
    pg_ref[0] = bins_ref[0, 0]
    pg_ref[1] = bins_ref[0, 1]
    copies[1].start()
    for cp in copies:
        cp.wait()


def local(dims, cotangent, amplitude, phase, position, profile, alt_weight):
    tables = jnp.asarray(make_tables())
    any_spec = pl.BlockSpec(memory_space=pl.ANY)
    vmem = pl.BlockSpec(memory_space=pltpu.VMEM)
    n_plane, n_column = dims[0] * dims[2], dims[1] * N_ALT
    dma = pltpu.SemaphoreType.DMA
    back, bins = pl.pallas_call(
        functools.partial(kernel, dims),
        out_shape=(pltpu.VMEM((LANES, LANES), F32), pltpu.VMEM((1, LANES), F32)),
        in_specs=[any_spec] * 7,
        out_specs=(vmem, vmem),
        scratch_shapes=[
            pltpu.VMEM((512, LANES), BF16), pltpu.VMEM((LANES, LANES), BF16), pltpu.VMEM((LANES, LANES), F32), pltpu.VMEM((2, LANES), F32),
            pltpu.VMEM(tables.shape, BF16), pltpu.SMEM((2,), F32), pltpu.SMEM((2,), F32),
            pltpu.VMEM((8, 32, 256), BF16), pltpu.VMEM((8, 16, LANES), BF16), pltpu.VMEM((8, 16, LANES), F32), pltpu.VMEM((1, LANES), F32),
            pltpu.VMEM((8, 32, 256), BF16), pltpu.VMEM((8, 16, LANES), BF16), pltpu.VMEM((8, 16, LANES), F32), pltpu.VMEM((8, 1, LANES), F32),
            pltpu.VMEM((8, 16, LANES), F32), pltpu.VMEM((8, 16, LANES), F32),
            pltpu.VMEM((n_column, 1, LANES), F32), pltpu.VMEM((n_plane, 1, LANES), F32),
            pltpu.VMEM((1, LANES), F32), pltpu.VMEM((1, LANES), F32),
            pltpu.VMEM((4, LANES, LANES), F32), pltpu.VMEM((4, LANES, 256), F32), pltpu.VMEM((2, 4, 64, LANES), F32),
            pltpu.VMEM((2, 256, LANES), F32), pltpu.VMEM((4, LANES, LANES), F32), pltpu.VMEM((4, 64, 256), F32),
            pltpu.VMEM((4, 64, 256), BF16), pltpu.VMEM((4, 2, 32, LANES), F32),
            pltpu.VMEM((8, 4, 64, LANES), F32), pltpu.VMEM((8, 4, 64, LANES), F32),
            pltpu.VMEM((LANES, LANES), F32), pltpu.VMEM((LANES, LANES), F32),
            pltpu.VMEM((2, 4, 64, LANES), F32),
            dma((7,)), dma((5,)), dma((5,)), dma((2,)), dma((2,)),
        ],
        compiler_params=pltpu.CompilerParams(collective_id=0, has_side_effects=True),
    )(cotangent, amplitude, phase, position, profile, alt_weight, tables)
    return pl.pallas_call(
        finish,
        out_shape=(jax.ShapeDtypeStruct((LANES, LANES), F32), jax.ShapeDtypeStruct((2,), F32)),
        in_specs=[vmem, vmem],
        out_specs=(any_spec, any_spec),
        scratch_shapes=[pltpu.SMEM((2,), F32), dma((2,))],
    )(*(pltpu.with_memory_space_constraint(v, pltpu.VMEM) for v in (back, bins)))


def solution(mesh):
    dims = {32: (4, 2, 4), 2: (2, 1, 1)}[mesh.shape["sub"]]
    placed = (P("alt", "sub"), P("alt", "sub"), P("alt", "sub"), P(None, "sub"), P("alt"), P("alt"))
    return jax.shard_map(
        functools.partial(local, dims), mesh=mesh, in_specs=placed, out_specs=(P("alt", "sub"), P("alt")), check_vma=False
    )
```

```python
import functools

import jax
import jax.numpy as jnp
import numpy as np
from jax import lax
from jax.experimental import pallas as pl
from jax.experimental.pallas import tpu as pltpu
from jax.sharding import PartitionSpec as P

F32 = jnp.float32
BF16 = jnp.bfloat16
MESH = pl.DeviceIdType.MESH

N_PUPIL = 32
N_FIELD = 64
N_BINS = 16
N_ALT = 8
LANES = 128


def split_np(m):
    hi = np.asarray(m, np.float32).astype(BF16)
    lo = (np.asarray(m, np.float64) - hi.astype(np.float64)).astype(np.float32).astype(BF16)
    return hi, lo


def make_tables():
    n = np.arange(N_FIELD)
    angle = 2.0 * np.pi / N_FIELD * (np.outer(n, n) % N_FIELD)
    cos, sin = np.cos(angle), np.sin(angle)
    eye = np.eye(4)
    half_c, half_s = cos[:, :N_PUPIL], sin[:, :N_PUPIL]
    kc, ks = np.kron(eye, half_c), np.kron(eye, half_s)
    w1 = np.block([[kc.T, -ks.T], [ks.T, kc.T]])
    w3 = np.block([[kc, ks]])
    w4 = w3.T
    w5 = np.block([[kc, ks], [-ks, kc]])
    a2 = np.block([[half_c, half_s], [-half_s, half_c]])
    a3 = np.vstack([half_c.T, half_s.T])
    a4 = np.block([[half_c, 0 * half_c], [0 * half_s, half_s]])
    a5 = np.block([[cos[:N_PUPIL], -sin[:N_PUPIL]], [sin[:N_PUPIL], cos[:N_PUPIL]]])
    blocks = []
    for w in (w1[:, :256], w1[:, 256:], w3, w4, w5[:256], w5[256:]):
        blocks += list(split_np(w))
    for a in (a2, a4, a3):
        hi, lo = split_np(a)
        blocks.append(np.concatenate([hi, hi, lo, np.zeros_like(lo)], axis=1))
    hi, lo = split_np(a5)
    blocks += [np.concatenate([hi, hi], axis=1), np.concatenate([lo, np.zeros_like(lo)], axis=1)]
    return np.concatenate(blocks, axis=0)


W1, W3, W4, W5 = (0, 512), 1024, 1536, (2048, 2560)
A2, A4, A3, A5 = 3072, 3200, 3328, 3392


def split(x):
    hi = x.astype(BF16)
    return hi, (x - hi.astype(F32)).astype(BF16)


def mm(a, b):
    return jnp.dot(a, b, preferred_element_type=F32)


def lane_mm(parts, tab, row):
    rows = parts[0].shape[0]
    w_hi, w_lo = tab[row : row + 256, :], tab[row + 256 : row + 512, :]
    both = mm(jnp.concatenate(parts, axis=0), w_hi)
    return both[:rows] + both[rows:] + mm(parts[0], w_lo)


def row_mm(table, x):
    hi, lo = split(x)
    return mm(table, jnp.concatenate([hi, lo, hi], axis=0))


def both_signs(v):
    c_re, c_im, s_re, s_im = v[:32, :LANES], v[:32, LANES:], v[32:, :LANES], v[32:, LANES:]
    return jnp.concatenate([c_re - s_im, c_re + s_im], axis=0), jnp.concatenate([c_im + s_re, c_im - s_re], axis=0)


def sincos(x):
    n = jnp.floor(x * (2.0 / np.pi) + 0.5)
    r = x - n * 1.5703125
    r = r - n * 4.837512969970703125e-4
    r = r - n * 7.54978995489188216e-8
    z = r * r
    s = ((-1.9515295891e-4 * z + 8.3321608736e-3) * z - 1.6666654611e-1) * z * r + r
    c = ((2.443315711809948e-5 * z - 1.388731625493765e-3) * z + 4.166664568298827e-2) * z * z - 0.5 * z + 1.0
    q = n.astype(jnp.int32)
    odd = (q & 1) == 1
    sv = jnp.where(odd, c, s)
    cv = jnp.where(odd, s, c)
    sv = jnp.where((q & 2) == 2, -sv, sv)
    cv = jnp.where(((q + 1) & 2) == 2, -cv, cv)
    return sv, cv


def swap4(x):
    lane = lax.broadcasted_iota(jnp.int32, x[0].shape, 1)
    keep0 = ((lane // 4) % 2) == 0
    keep1 = ((lane // 8) % 2) == 0

    def pair(a, b, shift, keep):
        return (
            jnp.where(keep, a, pltpu.roll(b, shift, 1)),
            jnp.where(keep, pltpu.roll(a, LANES - shift, 1), b),
        )

    y0, y1 = pair(x[0], x[1], 4, keep0)
    y2, y3 = pair(x[2], x[3], 4, keep0)
    z0, z2 = pair(y0, y2, 8, keep1)
    z1, z3 = pair(y1, y3, 8, keep1)
    return z0, z1, z2, z3


def far_first(n):
    return sorted(range(n), key=lambda o: -min(o, n - o))


def kernel(
    dims,
    cot_hbm, amp_hbm, ph_hbm, pos_hbm, prof_hbm, wt_hbm,
    tab_hbm,
    grad_ref, bins_ref,
    cot_in, amp_in, ph_in, pos_ref,
    tab, prof_ref, wt_ref,
    cot_send, amp_send, ph_send, small_send,
    cot_recv, amp_recv, ph_recv, small_recv,
    back_send, back_recv, st_a, st_b, row_a, row_b,
    yu, uf, bw, yg, cs, gf, yt, xt, ct, sn, er, ei, sf,
    load_sem, send_sem, recv_sem, sems_a, sems_b,
):
    ny, nz, nx = dims
    me = lax.axis_index("alt")
    sub = lax.axis_index("sub")
    x, yz = lax.rem(sub, nx), lax.div(sub, nx)
    y, zl = lax.div(yz, nz), lax.rem(yz, nz)
    core, high = lax.rem(me, 2), lax.div(me, 2)
    nh = N_ALT // 2
    at_high = [2 * lax.rem(high + o, nh) for o in range(nh)]
    at_core = [core, 1 - core]

    at_y = [lax.rem(y + o, ny) * (nz * nx) + zl * nx for o in range(ny)]
    at_x = [lax.rem(x + o, nx) for o in range(nx)]
    plane = [{"sub": at_y[oy] + at_x[ox]} for oy in far_first(ny) for ox in far_first(nx) if oy or ox]
    at_z = [y * (nz * nx) + lax.rem(zl + o, nz) * nx + x for o in range(nz)]
    column = [
        {"sub": at_z[oz], "alt": at_high[oh] + at_core[oc]}
        for oh in far_first(nh)
        for oz in range(nz)
        for oc in range(2)
        if oh or oz or oc
    ]
    my_plane = y * nx + x
    my_column = zl * N_ALT + me

    loads = []
    for src, dst in (
        (ph_hbm, ph_in), (amp_hbm, amp_in), (cot_hbm, cot_in), (pos_hbm, pos_ref),
        (prof_hbm, prof_ref), (wt_hbm, wt_ref), (tab_hbm, tab),
    ):
        loads.append(pltpu.make_async_copy(src, dst, load_sem.at[len(loads)]))
    for k in range(4):
        part = pl.ds(32 * k, 32)
        pltpu.make_async_copy(ph_hbm.at[part], ph_in.at[part], load_sem.at[0]).start()
    loads[1].start()

    barrier = pltpu.get_barrier_semaphore()
    for device in column + plane:
        pl.semaphore_signal(barrier, inc=1, device_id=device, device_id_type=MESH)

    for cp in loads[2:]:
        cp.start()

    loads[0].wait()
    t = jnp.concatenate(swap4([ph_in[32 * k : 32 * k + 32, :] for k in range(4)]), axis=0).T
    ph_send[...] = t.reshape(8, 16, LANES)
    loads[1].wait()
    amp = amp_in[...].astype(F32)
    t = jnp.concatenate(swap4([amp[32 * k : 32 * k + 32, :] for k in range(4)]), axis=0).T
    amp_send[...] = t.reshape(8, 16, LANES).astype(BF16)

    loads[2].wait()
    for half in range(2):
        z = swap4([cot_in[256 * half + 64 * k : 256 * half + 64 * k + 64, :].astype(F32) for k in range(4)])
        for u in range(2):
            t = jnp.concatenate([z[2 * u], z[2 * u + 1]], axis=0).T
            cot_send[:, 16 * half : 16 * half + 16, LANES * u : LANES * u + LANES] = t.reshape(8, 16, LANES).astype(BF16)
    loads[4].wait()
    loads[5].wait()
    row = lax.broadcasted_iota(jnp.int32, (8, LANES), 0)
    lane = lax.broadcasted_iota(jnp.int32, (8, LANES), 1)
    small = jnp.zeros((1, LANES), F32)
    for b in range(2):
        small = jnp.where(lane[:1] == 2 * me + b, prof_ref[b], small)
        small = jnp.where(lane[:1] == N_BINS + 2 * me + b, wt_ref[b], small)
    small_send[...] = small

    pl.semaphore_wait(barrier, len(plane) + len(column))

    order = [(2, 0), (2, 1), (1, 0), (3, 0), (1, 1), (3, 1), (0, 1)]
    kinds = ((small_send, small_recv), (ph_send, ph_recv), (amp_send, amp_recv), (cot_send, cot_recv), (back_send, back_recv))

    def peer_of(offset):
        return at_high[offset[0]] + at_core[offset[1]]

    def exchange(kind, offset):
        src, dst = kinds[kind]
        peer = peer_of(offset)
        return pltpu.make_async_remote_copy(
            src_ref=src if kind == 0 else src.at[peer],
            dst_ref=dst.at[me],
            send_sem=send_sem.at[kind],
            recv_sem=recv_sem.at[kind],
            device_id={"alt": peer},
            device_id_type=MESH,
        )

    def start(kind):
        for offset in order:
            exchange(kind, offset).start()

    def wait_in(kind):
        dst = kinds[kind][1].at[pl.ds(0, N_ALT - 1)]
        pltpu.make_async_copy(dst, dst, recv_sem.at[kind]).wait()

    def wait_out(kind):
        dst = kinds[kind][1].at[pl.ds(0, N_ALT - 1)]
        pltpu.make_async_copy(dst, dst, send_sem.at[kind]).wait()

    start(0)
    for offset in order:
        exchange(1, offset).start()
        exchange(2, offset).start()
    start(3)

    small_recv[me] = small
    ph_recv[me] = ph_send[me]
    amp_recv[me] = amp_send[me]
    cot_recv[me] = cot_send[me]

    src = lax.broadcasted_iota(jnp.int32, (LANES, 4 * LANES), 0)
    dst = lax.broadcasted_iota(jnp.int32, (LANES, 4 * LANES), 1)
    pick = (src == 16 * me + 4 * ((dst % LANES) // 32) + dst // LANES).astype(F32)
    loads[3].wait()
    pos = jnp.concatenate([pos_ref[...], jnp.zeros((6, LANES), F32)], axis=0)
    pos = jnp.dot(pos, pick, precision=lax.Precision.HIGHEST, preferred_element_type=F32)
    r64 = lax.broadcasted_iota(jnp.int32, (N_FIELD, LANES), 0)
    l64 = lax.broadcasted_iota(jnp.int32, (N_FIELD, LANES), 1)
    dr = jnp.where(r64 < 32, r64, 32 - r64).astype(F32)
    dc = (l64 % 32).astype(F32)
    twice = jnp.where(r64 == 32, 0.0, jnp.where(l64 % 32 == 0, 1.0, 2.0)).astype(F32)
    for g in range(4):
        px = pos[0:1, LANES * g : LANES * g + LANES]
        py = pos[1:2, LANES * g : LANES * g + LANES]
        s, c = sincos(0.05 * (px * dc + py * dr))
        c2, s2 = c * c - s * s, 2.0 * s * c
        for j in range(8):
            ct[j, g], sn[j, g] = c, s
            if j < 7:
                c, s = c * c2 - s * s2, s * c2 + c * s2

    r32 = lax.broadcasted_iota(jnp.int32, (32, LANES), 0)
    l32 = lax.broadcasted_iota(jnp.int32, (32, LANES), 1)
    step = 0.05 * (2 * (r32 % 8) + 1).astype(F32)
    at = l32 % 64
    dr_lane = jnp.where(at < 32, at, 32 - at).astype(F32)
    for g in range(4):
        here = l32 == 16 * me + 4 * (r32 // 8) + g
        y_row = jnp.sum(jnp.where(here, pos_ref[1:2, :], 0.0), axis=1, keepdims=True)
        s, c = sincos(step * y_row * dr_lane)
        hi, lo = split(jnp.concatenate([c, s], axis=0))
        yt[g, :, :LANES], yt[g, :, LANES:] = hi, lo
        s, c = sincos(step * pos[0:1, LANES * g : LANES * g + LANES] * (l32 % 32).astype(F32))
        own = r32 // 8 == l32 // 32
        xt[g, 0], xt[g, 1] = jnp.where(own, c, 0.0), jnp.where(own, s, 0.0)

    wait_in(0)
    bins = small_recv[0]
    for k in range(1, N_ALT):
        bins = bins + small_recv[k]
    prof = jnp.where(lane[:1] < N_BINS, bins, 0.0)
    wt = jnp.where(lane[:1] < N_BINS, pltpu.roll(bins, LANES - N_BINS, 1), 0.0)
    total = jnp.sum(prof, axis=1, keepdims=True)
    omega = prof * wt / total
    for g in range(4):
        re = jnp.zeros((N_FIELD, LANES), F32)
        im = jnp.zeros((N_FIELD, LANES), F32)
        for j in range(8):
            up, down = omega[:, 8 + j : 9 + j], omega[:, 7 - j : 8 - j]
            re = re + (up + down) * ct[j, g]
            im = im - (up - down) * sn[j, g]
        sf[0, g] = re * twice
        sf[1, g] = im * twice

    loads[6].wait()
    wait_in(1)
    s, c = sincos(ph_recv[...].reshape(LANES, LANES))
    er[...], ei[...] = c, s
    wait_in(2)
    c, s = er[...], ei[...]
    amp = amp_recv[...].astype(F32).reshape(LANES, LANES)
    e_re, e_im = amp * c, amp * s
    er[...] = e_re
    ei[...] = e_im
    e_both = split(jnp.concatenate([e_re, e_im], axis=1))
    for h in range(2):
        half = lane_mm(e_both, tab, W1[h])
        yu[2 * h], yu[2 * h + 1] = half[:, :LANES], half[:, LANES:]
    a2, a3 = tab[A2 : A2 + LANES, :192], tab[A3 : A3 + 64, :192]
    power = []
    for g in range(4):
        m = [yu.at[k][pl.ds(g, 32, stride=4), :] for k in range(4)]
        m = [jnp.concatenate([m[0], m[1]], axis=1), jnp.concatenate([m[2], m[3]], axis=1)]
        u = row_mm(a2, jnp.concatenate(m, axis=0))
        uf[g] = u
        power.append(u[:64] * u[:64] + u[64:] * u[64:])
    yb = lane_mm(split(jnp.concatenate(power, axis=0)), tab, W3)
    keep = twice * (1.0 / (1024.0 * 4096.0))
    for g in range(4):
        v = row_mm(a3, yb[64 * g : 64 * g + 64, :])
        b_re, b_im = both_signs(v)
        bw[0, g], bw[1, g] = b_re * keep, b_im * keep

    wait_in(3)
    cot = cot_recv[...].reshape(256, 256)
    parts = []
    yy = mm(cot, tab[W3 : W3 + 256, :]) + mm(cot, tab[W3 + 256 : W3 + 512, :])
    yg[0], yg[1] = yy[:, :LANES], yy[:, LANES:]
    for g in range(4):
        m = [yg.at[k][pl.ds(g, 64, stride=4), :] for k in range(2)]
        v = row_mm(a3, jnp.concatenate(m, axis=1))
        g_re, g_im = both_signs(v)
        b_re, b_im = bw[0, g], bw[1, g]
        hi, lo = split(jnp.concatenate([g_re * b_re + g_im * b_im, g_im * b_re - g_re * b_im], axis=1))
        m = mm(yt[g], jnp.concatenate([hi, lo, hi, lo], axis=0))
        parts.append((
            xt[g, 0] * m[:32, :LANES] - xt[g, 1] * m[32:, :LANES],
            xt[g, 1] * m[:32, LANES:] + xt[g, 0] * m[32:, LANES:],
        ))
        gf[g] = jnp.concatenate([g_re, g_im], axis=1)

    sums = []
    for k in range(2):
        acc = parts[0][k] + parts[1][k] + parts[2][k] + parts[3][k]
        acc = acc[:8] + acc[8:16] + acc[16:24] + acc[24:]
        sums.append(jnp.sum(acc, axis=1, keepdims=True))
    here = jnp.where(lane == 8 + row, sums[0] + sums[1], 0.0) + jnp.where(lane == 7 - row, sums[0] - sums[1], 0.0)
    mine = jnp.sum(here, axis=0, keepdims=True)
    row_a[...] = mine
    st_a[my_column] = mine

    def post(peers, me_slot, src, dst, sems):
        for device in peers:
            pltpu.make_async_remote_copy(
                src_ref=src, dst_ref=dst.at[me_slot], send_sem=sems.at[0], recv_sem=sems.at[1],
                device_id=device, device_id_type=MESH,
            ).start()

    def wait_all(peers, dst, sem):
        if peers:
            part = dst.at[pl.ds(0, len(peers))]
            pltpu.make_async_copy(part, part, sem).wait()

    post(column, my_column, row_a, st_a, sems_a)

    @pl.when(me >= 0)
    def _():
        z = []
        for g in range(4):
            g_re, g_im, s_re, s_im = gf[g, :, :LANES], gf[g, :, LANES:], sf[0, g], sf[1, g]
            v = jnp.concatenate([g_re * s_re - g_im * s_im, g_re * s_im + g_im * s_re], axis=1)
            v = row_mm(tab[A4 : A4 + LANES, :192], jnp.concatenate([v[:32] + v[32:], v[:32] - v[32:]], axis=0))
            z.append(jnp.concatenate([v[:64, :LANES] + v[64:, LANES:], v[:64, LANES:] - v[64:, :LANES]], axis=1))
        g_hat = lane_mm(split(jnp.concatenate(z, axis=0)), tab, W4)
        for g in range(4):
            gh = g_hat[64 * g : 64 * g + 64, :]
            v = jnp.concatenate([uf[g, :64, :] * gh, uf[g, 64:, :] * gh], axis=0)
            hi, lo = split(v)
            v = mm(tab[A5 : A5 + 64, :], jnp.concatenate([hi, lo], axis=0)) + mm(tab[A5 + 64 : A5 + 128, :LANES], hi)
            for k in range(2):
                cs.at[k][pl.ds(g, 32, stride=4), :] = v[:32, LANES * k : LANES * k + LANES]
                cs.at[2 + k][pl.ds(g, 32, stride=4), :] = v[32:, LANES * k : LANES * k + LANES]
        conv = sum(lane_mm(split(jnp.concatenate([cs[2 * h], cs[2 * h + 1]], axis=1)), tab, W5[h]) for h in range(2))
        grad = (er[...] * conv[:, LANES:] - ei[...] * conv[:, :LANES]) * (2.0 / (1024.0 * 4096.0))
        back_send[...] = grad.reshape(8, 16, LANES)
    start(4)
    back_recv[me] = back_send[me]

    wait_all(column, st_a, sems_a.at[1])
    acc = st_a[0]
    for k in range(1, nz * N_ALT):
        acc = acc + st_a[k]
    row_b[...] = acc
    st_b[my_plane] = acc
    post(plane, my_plane, row_b, st_b, sems_b)

    wait_in(4)
    m = back_recv[...].reshape(LANES, LANES).T
    rows = swap4([m[32 * k : 32 * k + 32, :] for k in range(4)])
    for k in range(4):
        grad_ref[32 * k : 32 * k + 32, :] = rows[k]

    wait_all(plane, st_b, sems_b.at[1])
    stat = st_b[0]
    for k in range(1, ny * nx):
        stat = stat + st_b[k]
    centre = jnp.sum(prof * wt * stat, axis=1, keepdims=True)
    pg = (wt * stat / total - centre / (total * total)) * (1.0 / (ny * nz * nx * LANES))
    own = [jnp.sum(jnp.where(lane[:1] == 2 * me + b, pg, 0.0), axis=1, keepdims=True) for b in range(2)]
    bins_ref[...] = jnp.where(lane[:1] == 0, own[0], own[1])

    for kind in range(5):
        wait_out(kind)
    wait_all(column, st_a, sems_a.at[0])
    wait_all(plane, st_b, sems_b.at[0])


def finish(grad_ref, bins_ref, out_hbm, pg_hbm, pg_ref, sems):
    copies = [pltpu.make_async_copy(grad_ref, out_hbm, sems.at[0]), pltpu.make_async_copy(pg_ref, pg_hbm, sems.at[1])]
    for k in range(4):
        part = pl.ds(32 * k, 32)
        pltpu.make_async_copy(grad_ref.at[part], out_hbm.at[part], sems.at[0]).start()
    pg_ref[0] = bins_ref[0, 0]
    pg_ref[1] = bins_ref[0, 1]
    copies[1].start()
    for cp in copies:
        cp.wait()


def local(dims, cotangent, amplitude, phase, position, profile, alt_weight):
    tables = jnp.asarray(make_tables())
    any_spec = pl.BlockSpec(memory_space=pl.ANY)
    vmem = pl.BlockSpec(memory_space=pltpu.VMEM)
    n_plane, n_column = dims[0] * dims[2], dims[1] * N_ALT
    dma = pltpu.SemaphoreType.DMA
    back, bins = pl.pallas_call(
        functools.partial(kernel, dims),
        out_shape=(pltpu.VMEM((LANES, LANES), F32), pltpu.VMEM((1, LANES), F32)),
        in_specs=[any_spec] * 7,
        out_specs=(vmem, vmem),
        scratch_shapes=[
            pltpu.VMEM((512, LANES), BF16), pltpu.VMEM((LANES, LANES), BF16), pltpu.VMEM((LANES, LANES), F32), pltpu.VMEM((2, LANES), F32),
            pltpu.VMEM(tables.shape, BF16), pltpu.SMEM((2,), F32), pltpu.SMEM((2,), F32),
            pltpu.VMEM((8, 32, 256), BF16), pltpu.VMEM((8, 16, LANES), BF16), pltpu.VMEM((8, 16, LANES), F32), pltpu.VMEM((1, LANES), F32),
            pltpu.VMEM((8, 32, 256), BF16), pltpu.VMEM((8, 16, LANES), BF16), pltpu.VMEM((8, 16, LANES), F32), pltpu.VMEM((8, 1, LANES), F32),
            pltpu.VMEM((8, 16, LANES), F32), pltpu.VMEM((8, 16, LANES), F32),
            pltpu.VMEM((n_column, 1, LANES), F32), pltpu.VMEM((n_plane, 1, LANES), F32),
            pltpu.VMEM((1, LANES), F32), pltpu.VMEM((1, LANES), F32),
            pltpu.VMEM((4, LANES, LANES), F32), pltpu.VMEM((4, LANES, 256), F32), pltpu.VMEM((2, 4, 64, LANES), F32),
            pltpu.VMEM((2, 256, LANES), F32), pltpu.VMEM((4, LANES, LANES), F32), pltpu.VMEM((4, 64, 256), F32),
            pltpu.VMEM((4, 64, 256), BF16), pltpu.VMEM((4, 2, 32, LANES), F32),
            pltpu.VMEM((8, 4, 64, LANES), F32), pltpu.VMEM((8, 4, 64, LANES), F32),
            pltpu.VMEM((LANES, LANES), F32), pltpu.VMEM((LANES, LANES), F32),
            pltpu.VMEM((2, 4, 64, LANES), F32),
            dma((7,)), dma((5,)), dma((5,)), dma((2,)), dma((2,)),
        ],
        compiler_params=pltpu.CompilerParams(collective_id=0, has_side_effects=True),
    )(cotangent, amplitude, phase, position, profile, alt_weight, tables)
    return pl.pallas_call(
        finish,
        out_shape=(jax.ShapeDtypeStruct((LANES, LANES), F32), jax.ShapeDtypeStruct((2,), F32)),
        in_specs=[vmem, vmem],
        out_specs=(any_spec, any_spec),
        scratch_shapes=[pltpu.SMEM((2,), F32), dma((2,))],
    )(*(pltpu.with_memory_space_constraint(v, pltpu.VMEM) for v in (back, bins)))


def solution(mesh):
    dims = {32: (4, 2, 4), 2: (2, 1, 1)}[mesh.shape["sub"]]
    placed = (P("alt", "sub"), P("alt", "sub"), P("alt", "sub"), P(None, "sub"), P("alt"), P("alt"))
    return jax.shard_map(
        functools.partial(local, dims), mesh=mesh, in_specs=placed, out_specs=(P("alt", "sub"), P("alt")), check_vma=False
    )
```

```python
import functools

import jax
import jax.numpy as jnp
import numpy as np
from jax import lax
from jax.experimental import pallas as pl
from jax.experimental.pallas import tpu as pltpu
from jax.sharding import PartitionSpec as P

F32 = jnp.float32
BF16 = jnp.bfloat16
MESH = pl.DeviceIdType.MESH

N_PUPIL = 32
N_FIELD = 64
N_BINS = 16
N_ALT = 8
LANES = 128


def split_np(m):
    hi = np.asarray(m, np.float32).astype(BF16)
    lo = (np.asarray(m, np.float64) - hi.astype(np.float64)).astype(np.float32).astype(BF16)
    return hi, lo


def make_tables():
    n = np.arange(N_FIELD)
    angle = 2.0 * np.pi / N_FIELD * (np.outer(n, n) % N_FIELD)
    cos, sin = np.cos(angle), np.sin(angle)
    eye = np.eye(4)
    half_c, half_s = cos[:, :N_PUPIL], sin[:, :N_PUPIL]
    kc, ks = np.kron(eye, half_c), np.kron(eye, half_s)
    w1 = np.block([[kc.T, -ks.T], [ks.T, kc.T]])
    w3 = np.block([[kc, ks]])
    w4 = w3.T
    w5 = np.block([[kc, ks], [-ks, kc]])
    a2 = np.block([[half_c, half_s], [-half_s, half_c]])
    a3 = np.vstack([half_c.T, half_s.T])
    a4 = np.block([[half_c, 0 * half_c], [0 * half_s, half_s]])
    a5 = np.block([[cos[:N_PUPIL], -sin[:N_PUPIL]], [sin[:N_PUPIL], cos[:N_PUPIL]]])
    blocks = []
    for w in (w1[:, :256], w1[:, 256:], w3, w4, w5[:256], w5[256:]):
        blocks += list(split_np(w))
    for a in (a2, a4, a3):
        hi, lo = split_np(a)
        blocks.append(np.concatenate([hi, hi, lo, np.zeros_like(lo)], axis=1))
    hi, lo = split_np(a5)
    blocks += [np.concatenate([hi, hi], axis=1), np.concatenate([lo, np.zeros_like(lo)], axis=1)]
    return np.concatenate(blocks, axis=0)


W1, W3, W4, W5 = (0, 512), 1024, 1536, (2048, 2560)
A2, A4, A3, A5 = 3072, 3200, 3328, 3392


def split(x):
    hi = x.astype(BF16)
    return hi, (x - hi.astype(F32)).astype(BF16)


def mm(a, b):
    return jnp.dot(a, b, preferred_element_type=F32)


def lane_mm(parts, tab, row):
    rows = parts[0].shape[0]
    w_hi, w_lo = tab[row : row + 256, :], tab[row + 256 : row + 512, :]
    both = mm(jnp.concatenate(parts, axis=0), w_hi)
    return both[:rows] + both[rows:] + mm(parts[0], w_lo)


def row_mm(table, x):
    hi, lo = split(x)
    return mm(table, jnp.concatenate([hi, lo, hi], axis=0))


def both_signs(v):
    c_re, c_im, s_re, s_im = v[:32, :LANES], v[:32, LANES:], v[32:, :LANES], v[32:, LANES:]
    return jnp.concatenate([c_re - s_im, c_re + s_im], axis=0), jnp.concatenate([c_im + s_re, c_im - s_re], axis=0)


def sincos(x):
    n = jnp.floor(x * (2.0 / np.pi) + 0.5)
    r = x - n * 1.5703125
    r = r - n * 4.837512969970703125e-4
    r = r - n * 7.54978995489188216e-8
    z = r * r
    s = ((-1.9515295891e-4 * z + 8.3321608736e-3) * z - 1.6666654611e-1) * z * r + r
    c = ((2.443315711809948e-5 * z - 1.388731625493765e-3) * z + 4.166664568298827e-2) * z * z - 0.5 * z + 1.0
    q = n.astype(jnp.int32)
    odd = (q & 1) == 1
    sv = jnp.where(odd, c, s)
    cv = jnp.where(odd, s, c)
    sv = jnp.where((q & 2) == 2, -sv, sv)
    cv = jnp.where(((q + 1) & 2) == 2, -cv, cv)
    return sv, cv


def swap4(x):
    lane = lax.broadcasted_iota(jnp.int32, x[0].shape, 1)
    keep0 = ((lane // 4) % 2) == 0
    keep1 = ((lane // 8) % 2) == 0

    def pair(a, b, shift, keep):
        return (
            jnp.where(keep, a, pltpu.roll(b, shift, 1)),
            jnp.where(keep, pltpu.roll(a, LANES - shift, 1), b),
        )

    y0, y1 = pair(x[0], x[1], 4, keep0)
    y2, y3 = pair(x[2], x[3], 4, keep0)
    z0, z2 = pair(y0, y2, 8, keep1)
    z1, z3 = pair(y1, y3, 8, keep1)
    return z0, z1, z2, z3


def far_first(n):
    return sorted(range(n), key=lambda o: -min(o, n - o))


def kernel(
    dims,
    cot_hbm, amp_hbm, ph_hbm, pos_hbm, prof_hbm, wt_hbm,
    tab_hbm,
    grad_ref, bins_ref,
    cot_in, amp_in, ph_in, pos_ref,
    tab, prof_ref, wt_ref,
    cot_send, amp_send, ph_send, small_send,
    cot_recv, amp_recv, ph_recv, small_recv,
    back_send, back_recv, st_a, st_b, row_a, row_b,
    yu, uf, bw, yg, cs, gf, yt, xt, ct, sn, er, ei, sf,
    load_sem, send_sem, recv_sem, sems_a, sems_b,
):
    ny, nz, nx = dims
    me = lax.axis_index("alt")
    sub = lax.axis_index("sub")
    x, yz = lax.rem(sub, nx), lax.div(sub, nx)
    y, zl = lax.div(yz, nz), lax.rem(yz, nz)
    core, high = lax.rem(me, 2), lax.div(me, 2)
    nh = N_ALT // 2
    at_high = [2 * lax.rem(high + o, nh) for o in range(nh)]
    at_core = [core, 1 - core]

    at_y = [lax.rem(y + o, ny) * (nz * nx) + zl * nx for o in range(ny)]
    at_x = [lax.rem(x + o, nx) for o in range(nx)]
    plane = [{"sub": at_y[oy] + at_x[ox]} for oy in far_first(ny) for ox in far_first(nx) if oy or ox]
    at_z = [y * (nz * nx) + lax.rem(zl + o, nz) * nx + x for o in range(nz)]
    column = [
        {"sub": at_z[oz], "alt": at_high[oh] + at_core[oc]}
        for oh in far_first(nh)
        for oz in range(nz)
        for oc in range(2)
        if oh or oz or oc
    ]
    my_plane = y * nx + x
    my_column = zl * N_ALT + me

    loads = []
    for src, dst in (
        (ph_hbm, ph_in), (amp_hbm, amp_in), (cot_hbm, cot_in), (pos_hbm, pos_ref),
        (prof_hbm, prof_ref), (wt_hbm, wt_ref), (tab_hbm, tab),
    ):
        loads.append(pltpu.make_async_copy(src, dst, load_sem.at[len(loads)]))
    for k in range(4):
        part = pl.ds(32 * k, 32)
        pltpu.make_async_copy(ph_hbm.at[part], ph_in.at[part], load_sem.at[0]).start()
    loads[1].start()

    barrier = pltpu.get_barrier_semaphore()
    for device in column + plane:
        pl.semaphore_signal(barrier, inc=1, device_id=device, device_id_type=MESH)

    for cp in loads[2:]:
        cp.start()

    loads[0].wait()
    t = jnp.concatenate(swap4([ph_in[32 * k : 32 * k + 32, :] for k in range(4)]), axis=0).T
    ph_send[...] = t.reshape(8, 16, LANES)
    loads[1].wait()
    amp = amp_in[...].astype(F32)
    t = jnp.concatenate(swap4([amp[32 * k : 32 * k + 32, :] for k in range(4)]), axis=0).T
    amp_send[...] = t.reshape(8, 16, LANES).astype(BF16)

    loads[2].wait()
    for half in range(2):
        z = swap4([cot_in[256 * half + 64 * k : 256 * half + 64 * k + 64, :].astype(F32) for k in range(4)])
        for u in range(2):
            t = jnp.concatenate([z[2 * u], z[2 * u + 1]], axis=0).T
            cot_send[:, 16 * half : 16 * half + 16, LANES * u : LANES * u + LANES] = t.reshape(8, 16, LANES).astype(BF16)
    loads[4].wait()
    loads[5].wait()
    row = lax.broadcasted_iota(jnp.int32, (8, LANES), 0)
    lane = lax.broadcasted_iota(jnp.int32, (8, LANES), 1)
    small = jnp.zeros((1, LANES), F32)
    for b in range(2):
        small = jnp.where(lane[:1] == 2 * me + b, prof_ref[b], small)
        small = jnp.where(lane[:1] == N_BINS + 2 * me + b, wt_ref[b], small)
    small_send[...] = small

    pl.semaphore_wait(barrier, len(plane) + len(column))

    order = [(2, 0), (2, 1), (1, 0), (3, 0), (1, 1), (3, 1), (0, 1)]
    kinds = ((small_send, small_recv), (ph_send, ph_recv), (amp_send, amp_recv), (cot_send, cot_recv), (back_send, back_recv))

    def peer_of(offset):
        return at_high[offset[0]] + at_core[offset[1]]

    def exchange(kind, offset):
        src, dst = kinds[kind]
        peer = peer_of(offset)
        return pltpu.make_async_remote_copy(
            src_ref=src if kind == 0 else src.at[peer],
            dst_ref=dst.at[me],
            send_sem=send_sem.at[kind],
            recv_sem=recv_sem.at[kind],
            device_id={"alt": peer},
            device_id_type=MESH,
        )

    def start(kind):
        for offset in order:
            exchange(kind, offset).start()

    def wait_in(kind):
        dst = kinds[kind][1].at[pl.ds(0, N_ALT - 1)]
        pltpu.make_async_copy(dst, dst, recv_sem.at[kind]).wait()

    def wait_out(kind):
        dst = kinds[kind][1].at[pl.ds(0, N_ALT - 1)]
        pltpu.make_async_copy(dst, dst, send_sem.at[kind]).wait()

    start(0)
    for offset in order:
        exchange(1, offset).start()
        exchange(2, offset).start()
    start(3)

    small_recv[me] = small
    ph_recv[me] = ph_send[me]
    amp_recv[me] = amp_send[me]
    cot_recv[me] = cot_send[me]

    src = lax.broadcasted_iota(jnp.int32, (LANES, 4 * LANES), 0)
    dst = lax.broadcasted_iota(jnp.int32, (LANES, 4 * LANES), 1)
    pick = (src == 16 * me + 4 * ((dst % LANES) // 32) + dst // LANES).astype(F32)
    loads[3].wait()
    pos = jnp.concatenate([pos_ref[...], jnp.zeros((6, LANES), F32)], axis=0)
    pos = jnp.dot(pos, pick, precision=lax.Precision.HIGHEST, preferred_element_type=F32)
    r64 = lax.broadcasted_iota(jnp.int32, (N_FIELD, LANES), 0)
    l64 = lax.broadcasted_iota(jnp.int32, (N_FIELD, LANES), 1)
    dr = jnp.where(r64 < 32, r64, 32 - r64).astype(F32)
    dc = (l64 % 32).astype(F32)
    twice = jnp.where(r64 == 32, 0.0, jnp.where(l64 % 32 == 0, 1.0, 2.0)).astype(F32)
    for g in range(4):
        px = pos[0:1, LANES * g : LANES * g + LANES]
        py = pos[1:2, LANES * g : LANES * g + LANES]
        s, c = sincos(0.05 * (px * dc + py * dr))
        c2, s2 = c * c - s * s, 2.0 * s * c
        for j in range(8):
            ct[j, g], sn[j, g] = c, s
            if j < 7:
                c, s = c * c2 - s * s2, s * c2 + c * s2

    r32 = lax.broadcasted_iota(jnp.int32, (32, LANES), 0)
    l32 = lax.broadcasted_iota(jnp.int32, (32, LANES), 1)
    step = 0.05 * (2 * (r32 % 8) + 1).astype(F32)
    at = l32 % 64
    dr_lane = jnp.where(at < 32, at, 32 - at).astype(F32)
    for g in range(4):
        here = l32 == 16 * me + 4 * (r32 // 8) + g
        y_row = jnp.sum(jnp.where(here, pos_ref[1:2, :], 0.0), axis=1, keepdims=True)
        s, c = sincos(step * y_row * dr_lane)
        hi, lo = split(jnp.concatenate([c, s], axis=0))
        yt[g, :, :LANES], yt[g, :, LANES:] = hi, lo
        s, c = sincos(step * pos[0:1, LANES * g : LANES * g + LANES] * (l32 % 32).astype(F32))
        own = r32 // 8 == l32 // 32
        xt[g, 0], xt[g, 1] = jnp.where(own, c, 0.0), jnp.where(own, s, 0.0)

    wait_in(0)
    bins = small_recv[0]
    for k in range(1, N_ALT):
        bins = bins + small_recv[k]
    prof = jnp.where(lane[:1] < N_BINS, bins, 0.0)
    wt = jnp.where(lane[:1] < N_BINS, pltpu.roll(bins, LANES - N_BINS, 1), 0.0)
    total = jnp.sum(prof, axis=1, keepdims=True)
    omega = prof * wt / total
    for g in range(4):
        re = jnp.zeros((N_FIELD, LANES), F32)
        im = jnp.zeros((N_FIELD, LANES), F32)
        for j in range(8):
            up, down = omega[:, 8 + j : 9 + j], omega[:, 7 - j : 8 - j]
            re = re + (up + down) * ct[j, g]
            im = im - (up - down) * sn[j, g]
        sf[0, g] = re * twice
        sf[1, g] = im * twice

    loads[6].wait()
    wait_in(1)
    s, c = sincos(ph_recv[...].reshape(LANES, LANES))
    er[...], ei[...] = c, s
    wait_in(2)
    c, s = er[...], ei[...]
    amp = amp_recv[...].astype(F32).reshape(LANES, LANES)
    e_re, e_im = amp * c, amp * s
    er[...] = e_re
    ei[...] = e_im
    e_both = split(jnp.concatenate([e_re, e_im], axis=1))
    for h in range(2):
        half = lane_mm(e_both, tab, W1[h])
        yu[2 * h], yu[2 * h + 1] = half[:, :LANES], half[:, LANES:]
    a2, a3 = tab[A2 : A2 + LANES, :192], tab[A3 : A3 + 64, :192]
    power = []
    for g in range(4):
        m = [yu.at[k][pl.ds(g, 32, stride=4), :] for k in range(4)]
        m = [jnp.concatenate([m[0], m[1]], axis=1), jnp.concatenate([m[2], m[3]], axis=1)]
        u = row_mm(a2, jnp.concatenate(m, axis=0))
        uf[g] = u
        power.append(u[:64] * u[:64] + u[64:] * u[64:])
    yb = lane_mm(split(jnp.concatenate(power, axis=0)), tab, W3)
    keep = twice * (1.0 / (1024.0 * 4096.0))
    for g in range(4):
        v = row_mm(a3, yb[64 * g : 64 * g + 64, :])
        b_re, b_im = both_signs(v)
        bw[0, g], bw[1, g] = b_re * keep, b_im * keep

    wait_in(3)
    cot = cot_recv[...].reshape(256, 256)
    parts = []
    yy = mm(cot, tab[W3 : W3 + 256, :]) + mm(cot, tab[W3 + 256 : W3 + 512, :])
    yg[0], yg[1] = yy[:, :LANES], yy[:, LANES:]
    for g in range(4):
        m = [yg.at[k][pl.ds(g, 64, stride=4), :] for k in range(2)]
        v = row_mm(a3, jnp.concatenate(m, axis=1))
        g_re, g_im = both_signs(v)
        b_re, b_im = bw[0, g], bw[1, g]
        hi, lo = split(jnp.concatenate([g_re * b_re + g_im * b_im, g_im * b_re - g_re * b_im], axis=1))
        m = mm(yt[g], jnp.concatenate([hi, lo, hi, lo], axis=0))
        parts.append((
            xt[g, 0] * m[:32, :LANES] - xt[g, 1] * m[32:, :LANES],
            xt[g, 1] * m[:32, LANES:] + xt[g, 0] * m[32:, LANES:],
        ))
        gf[g] = jnp.concatenate([g_re, g_im], axis=1)

    sums = []
    for k in range(2):
        acc = parts[0][k] + parts[1][k] + parts[2][k] + parts[3][k]
        acc = acc[:8] + acc[8:16] + acc[16:24] + acc[24:]
        sums.append(jnp.sum(acc, axis=1, keepdims=True))
    here = jnp.where(lane == 8 + row, sums[0] + sums[1], 0.0) + jnp.where(lane == 7 - row, sums[0] - sums[1], 0.0)
    mine = jnp.sum(here, axis=0, keepdims=True)
    row_a[...] = mine
    st_a[my_column] = mine

    def post(peers, me_slot, src, dst, sems):
        for device in peers:
            pltpu.make_async_remote_copy(
                src_ref=src, dst_ref=dst.at[me_slot], send_sem=sems.at[0], recv_sem=sems.at[1],
                device_id=device, device_id_type=MESH,
            ).start()

    def wait_all(peers, dst, sem):
        if peers:
            part = dst.at[pl.ds(0, len(peers))]
            pltpu.make_async_copy(part, part, sem).wait()

    post(column, my_column, row_a, st_a, sems_a)

    @pl.when(me >= 0)
    def _():
        z = []
        for g in range(4):
            g_re, g_im, s_re, s_im = gf[g, :, :LANES], gf[g, :, LANES:], sf[0, g], sf[1, g]
            v = jnp.concatenate([g_re * s_re - g_im * s_im, g_re * s_im + g_im * s_re], axis=1)
            v = row_mm(tab[A4 : A4 + LANES, :192], jnp.concatenate([v[:32] + v[32:], v[:32] - v[32:]], axis=0))
            z.append(jnp.concatenate([v[:64, :LANES] + v[64:, LANES:], v[:64, LANES:] - v[64:, :LANES]], axis=1))
        g_hat = lane_mm(split(jnp.concatenate(z, axis=0)), tab, W4)
        for g in range(4):
            gh = g_hat[64 * g : 64 * g + 64, :]
            v = jnp.concatenate([uf[g, :64, :] * gh, uf[g, 64:, :] * gh], axis=0)
            hi, lo = split(v)
            v = mm(tab[A5 : A5 + 64, :], jnp.concatenate([hi, lo], axis=0)) + mm(tab[A5 + 64 : A5 + 128, :LANES], hi)
            for k in range(2):
                cs.at[k][pl.ds(g, 32, stride=4), :] = v[:32, LANES * k : LANES * k + LANES]
                cs.at[2 + k][pl.ds(g, 32, stride=4), :] = v[32:, LANES * k : LANES * k + LANES]
        conv = sum(lane_mm(split(jnp.concatenate([cs[2 * h], cs[2 * h + 1]], axis=1)), tab, W5[h]) for h in range(2))
        grad = (er[...] * conv[:, LANES:] - ei[...] * conv[:, :LANES]) * (2.0 / (1024.0 * 4096.0))
        back_send[...] = grad.reshape(8, 16, LANES)
    start(4)
    back_recv[me] = back_send[me]

    wait_all(column, st_a, sems_a.at[1])
    acc = st_a[0]
    for k in range(1, nz * N_ALT):
        acc = acc + st_a[k]
    row_b[...] = acc
    st_b[my_plane] = acc
    post(plane, my_plane, row_b, st_b, sems_b)

    wait_in(4)
    m = back_recv[...].reshape(LANES, LANES).T
    rows = swap4([m[32 * k : 32 * k + 32, :] for k in range(4)])
    for k in range(4):
        grad_ref[32 * k : 32 * k + 32, :] = rows[k]

    for kind in range(5):
        wait_out(kind)
    wait_all(column, st_a, sems_a.at[0])
    wait_all(plane, st_b, sems_b.at[1])
    stat = st_b[0]
    for k in range(1, ny * nx):
        stat = stat + st_b[k]
    centre = jnp.sum(prof * wt * stat, axis=1, keepdims=True)
    pg = (wt * stat / total - centre / (total * total)) * (1.0 / (ny * nz * nx * LANES))
    own = [jnp.sum(jnp.where(lane[:1] == 2 * me + b, pg, 0.0), axis=1, keepdims=True) for b in range(2)]
    bins_ref[...] = jnp.where(lane[:1] == 0, own[0], own[1])

    wait_all(plane, st_b, sems_b.at[0])


def finish(grad_ref, bins_ref, out_hbm, pg_hbm, pg_ref, sems):
    copies = [pltpu.make_async_copy(grad_ref, out_hbm, sems.at[0]), pltpu.make_async_copy(pg_ref, pg_hbm, sems.at[1])]
    for k in range(4):
        part = pl.ds(32 * k, 32)
        pltpu.make_async_copy(grad_ref.at[part], out_hbm.at[part], sems.at[0]).start()
    pg_ref[0] = bins_ref[0, 0]
    pg_ref[1] = bins_ref[0, 1]
    copies[1].start()
    for cp in copies:
        cp.wait()


def local(dims, cotangent, amplitude, phase, position, profile, alt_weight):
    tables = jnp.asarray(make_tables())
    any_spec = pl.BlockSpec(memory_space=pl.ANY)
    vmem = pl.BlockSpec(memory_space=pltpu.VMEM)
    n_plane, n_column = dims[0] * dims[2], dims[1] * N_ALT
    dma = pltpu.SemaphoreType.DMA
    back, bins = pl.pallas_call(
        functools.partial(kernel, dims),
        out_shape=(pltpu.VMEM((LANES, LANES), F32), pltpu.VMEM((1, LANES), F32)),
        in_specs=[any_spec] * 7,
        out_specs=(vmem, vmem),
        scratch_shapes=[
            pltpu.VMEM((512, LANES), BF16), pltpu.VMEM((LANES, LANES), BF16), pltpu.VMEM((LANES, LANES), F32), pltpu.VMEM((2, LANES), F32),
            pltpu.VMEM(tables.shape, BF16), pltpu.SMEM((2,), F32), pltpu.SMEM((2,), F32),
            pltpu.VMEM((8, 32, 256), BF16), pltpu.VMEM((8, 16, LANES), BF16), pltpu.VMEM((8, 16, LANES), F32), pltpu.VMEM((1, LANES), F32),
            pltpu.VMEM((8, 32, 256), BF16), pltpu.VMEM((8, 16, LANES), BF16), pltpu.VMEM((8, 16, LANES), F32), pltpu.VMEM((8, 1, LANES), F32),
            pltpu.VMEM((8, 16, LANES), F32), pltpu.VMEM((8, 16, LANES), F32),
            pltpu.VMEM((n_column, 1, LANES), F32), pltpu.VMEM((n_plane, 1, LANES), F32),
            pltpu.VMEM((1, LANES), F32), pltpu.VMEM((1, LANES), F32),
            pltpu.VMEM((4, LANES, LANES), F32), pltpu.VMEM((4, LANES, 256), F32), pltpu.VMEM((2, 4, 64, LANES), F32),
            pltpu.VMEM((2, 256, LANES), F32), pltpu.VMEM((4, LANES, LANES), F32), pltpu.VMEM((4, 64, 256), F32),
            pltpu.VMEM((4, 64, 256), BF16), pltpu.VMEM((4, 2, 32, LANES), F32),
            pltpu.VMEM((8, 4, 64, LANES), F32), pltpu.VMEM((8, 4, 64, LANES), F32),
            pltpu.VMEM((LANES, LANES), F32), pltpu.VMEM((LANES, LANES), F32),
            pltpu.VMEM((2, 4, 64, LANES), F32),
            dma((7,)), dma((5,)), dma((5,)), dma((2,)), dma((2,)),
        ],
        compiler_params=pltpu.CompilerParams(collective_id=0, has_side_effects=True),
    )(cotangent, amplitude, phase, position, profile, alt_weight, tables)
    return pl.pallas_call(
        finish,
        out_shape=(jax.ShapeDtypeStruct((LANES, LANES), F32), jax.ShapeDtypeStruct((2,), F32)),
        in_specs=[vmem, vmem],
        out_specs=(any_spec, any_spec),
        scratch_shapes=[pltpu.SMEM((2,), F32), dma((2,))],
    )(*(pltpu.with_memory_space_constraint(v, pltpu.VMEM) for v in (back, bins)))


def solution(mesh):
    dims = {32: (4, 2, 4), 2: (2, 1, 1)}[mesh.shape["sub"]]
    placed = (P("alt", "sub"), P("alt", "sub"), P("alt", "sub"), P(None, "sub"), P("alt"), P("alt"))
    return jax.shard_map(
        functools.partial(local, dims), mesh=mesh, in_specs=placed, out_specs=(P("alt", "sub"), P("alt")), check_vma=False
    )
```
